32 devices in a mesh: dp: 8 (over z, y), grad: 4 (over x, core).
Axes of the slice: x: 2, y: 2, z: 4, core: 2. Of those that a mesh axis runs over, the one named last changes fastest.
Arguments:
- activations: bfloat16 [2048, 5120], P('dp', 'grad')
- grad_rows: bfloat16 [41472, 5120], P(('grad', 'dp')), may hold values from -6 to 6
- live_rows: int32 [4], P('grad'), may hold values from 1 to 10368, 27648 in all
Outputs:
- preconditioned: float32 [41472, 5120], P(('grad', 'dp'))
The draws below stay inside these ranges and needn't reach their ends.
Inputs may be any that keep to these rules, and one draw needn't show every extreme that they name: `live_rows`: the counts sum to 27648, and one worker's count is exactly 10368.
All inputs are finite; a program needn't handle non-finite values. No bound on the sum of `live_rows` on one device may be relied on, other than what follows from the above.
Results may differ from the reference program's by a relative error of at most 0.0003.
Values sent between devices are 32-bit elements; how exact they have to be, the bound alone decides.
No kernel may reach another device: no remote copies, remote signals or barrier semaphores. Data moves between devices by JAX's collectives and lax.ppermute only.
A program may use at most 128 MiB of HBM per device.

```python
import math
import jax
import jax.numpy as jnp
import numpy as np
from jax import lax

D = 5120
FF = 13824
BLK = 160
TOKENS = 2048
SLOTS = 41472
CAP = 10368
N_GRAD = 4


def draw_activations(key, part):
    subkeys = jax.random.split(jax.random.fold_in(key, 11), 3)
    noise_wide = jax.random.normal(subkeys[0], (TOKENS, D + 3), jnp.float32)
    banded = noise_wide[:, :D] + 0.7 * noise_wide[:, 1:D + 1] - 0.5 * noise_wide[:, 3:D + 3]
    feature_spread = jnp.exp(jax.random.uniform(subkeys[1], (1, D), jnp.float32, math.log(0.7), math.log(1.4)))
    feature_rising = 0.6 * jnp.exp(math.log(3.0) * jnp.arange(D, dtype=jnp.float32)[None, :] / D)
    token_spread = jnp.exp(jax.random.uniform(subkeys[2], (TOKENS, 1), jnp.float32, math.log(0.6), math.log(1.2)))
    token_rising = jnp.exp(math.log(3.0) * jnp.arange(TOKENS, dtype=jnp.float32)[:, None] / TOKENS)
    return (banded * feature_spread * feature_rising * token_spread * token_rising).astype(jnp.bfloat16)


def shard_levels(own_key, shape, shards, low, high):
    factor_of = 1.0
    for axis_at, shards_of in shards:
        steps = jax.random.uniform(jax.random.fold_in(jax.random.fold_in(own_key, 6), axis_at), (shards_of,), jnp.float32, low / len(shards), high / len(shards))
        factor_of = factor_of * jnp.repeat(jnp.exp(steps), shape[axis_at] // shards_of).reshape((-1,) + (1,) * (len(shape) - 1 - axis_at))
    return factor_of


def length_profile(amount, total, bound, lean):
    loads = [(1 << 20) // math.isqrt(rank ** lean) + 1 for rank in range(2, amount + 1)]
    rest, counts = total - bound - (amount - 1), [1] * (amount - 1)
    while rest > 0:
        movable = [i for i in range(amount - 1) if counts[i] < bound]
        mass, remaining = sum([loads[i] for i in movable]), rest
        for i in movable:
            extra = min(bound - counts[i], max(1, remaining * loads[i] // mass), rest)
            counts[i] = counts[i] + extra
            rest = rest - extra
    return np.array([bound] + counts)


def uneven_parts(rng, amount, total, reach, skew):
    if amount == 2:
        one = jax.random.randint(rng, (), max(1, total - reach), min(reach, total - 1) + 1)
        return jnp.stack([one, total - one])
    tallies = jnp.asarray(length_profile(amount, total, reach, skew), jnp.int32)
    couples = (amount - 1) // 2
    source_of, sink = tallies[1:1 + 2 * couples:2], tallies[2:2 + 2 * couples:2]
    margin = jnp.minimum(source_of - 1, reach - sink)
    shifted = jax.random.randint(jax.random.fold_in(rng, 1), (couples,), 0, 1 << 20) % (margin + 1)
    tallies = tallies.at[1:1 + 2 * couples:2].set(source_of - shifted).at[2:2 + 2 * couples:2].set(sink + shifted)
    return tallies[jax.random.permutation(jax.random.fold_in(rng, 2), amount)]


def normal_values(key, dims, scale, most, pieces=(), kind=jnp.bfloat16):
    array = jax.random.normal(key, dims, jnp.float32) * scale
    if len(pieces) > 0:
        array = shard_levels(key, dims, pieces, -0.22, 0.18) * array
    return jnp.clip(array, min=-most, max=most).astype(kind)


def setup_inputs(seed: int = 0) -> dict:
    key_of = jax.random.split(jax.random.key(seed), 4)
    activations = draw_activations(jax.random.fold_in(key_of[3], 71), 0)
    grad_rows = normal_values(key_of[1], (SLOTS, D), 1.0, 6.0, ((0, 32),))
    live_rows = uneven_parts(key_of[2], N_GRAD, 2 * FF, CAP, 2).astype(jnp.int32)
    return {"activations": activations, "grad_rows": grad_rows, "live_rows": live_rows}


def reference(activations, grad_rows, live_rows):
    count_tokens = activations.shape[0]
    block_count = D // BLK

    def block_stat(block_index):
        column_piece = lax.dynamic_slice_in_dim(activations, block_index * BLK, BLK, 1)
        product = jnp.dot(column_piece.T.astype(jnp.float32), column_piece.astype(jnp.float32), preferred_element_type=jnp.float32)
        return product * (1.0 / count_tokens)
    statistics = lax.map(block_stat, jnp.arange(block_count, dtype=jnp.int32))
    diag_total = jnp.sum(jnp.diagonal(statistics, axis1=1, axis2=2))
    level = 0.5 * diag_total / D + 1e-06
    identity = jnp.eye(BLK, dtype=jnp.float32)[None, :, :]
    factors = jnp.linalg.cholesky(statistics + level * identity)
    lower_inv = lax.linalg.triangular_solve(factors, jnp.broadcast_to(identity, factors.shape), left_side=True, lower=True)
    inverses = jnp.einsum('kji,kjl->kil', lower_inv, lower_inv, precision=lax.Precision.HIGHEST)

    def apply_block(block_index):
        column_piece = lax.dynamic_slice_in_dim(grad_rows, block_index * BLK, BLK, 1).astype(jnp.float32)
        return jnp.dot(column_piece, inverses[block_index], precision=lax.Precision.HIGHEST)
    solved = lax.map(apply_block, jnp.arange(block_count, dtype=jnp.int32))
    result = jnp.transpose(solved, (1, 0, 2)).reshape(grad_rows.shape[0], D)
    slot_index = jnp.arange(grad_rows.shape[0], dtype=jnp.int32)
    per_worker = grad_rows.shape[0] // N_GRAD
    worker = slot_index // per_worker
    live_mask = slot_index % per_worker < live_rows[worker]
    return jnp.where(live_mask[:, None], result, jnp.zeros_like(result))
```

```python
import functools

import jax
import jax.numpy as jnp
from jax import lax
from jax.experimental import pallas as pl
from jax.experimental.pallas import tpu as pltpu
from jax.sharding import PartitionSpec as P

D = 5120
BLK = 160
MAIN = 128
REST = BLK - MAIN
HALF = 64
ROWS = 104
GROUP = 4
WIDE = GROUP * BLK
TRACE_LANE = 72
VMEM = pl.BlockSpec(memory_space=pltpu.VMEM)
SMEM = pl.BlockSpec(memory_space=pltpu.SMEM)
HIGHEST = lax.Precision.HIGHEST


def iota(shape, dim):
    return lax.broadcasted_iota(jnp.int32, shape, dim)


def dot(a, b, ca, cb, precision=None):
    return lax.dot_general(
        a, b, (((ca,), (cb,)), ((), ())), precision=precision, preferred_element_type=jnp.float32
    )


def pack(b11, b21, b22, trace):
    top, low = b11[:HALF], pltpu.roll(b11[HALF:], HALF, 1)
    lane, row = iota((HALF, MAIN), 1), iota((HALF, MAIN), 0)
    first = jnp.where(lane < row, low, top)
    first = jnp.where(lane < HALF, first, top)
    diagonal = jnp.sum(jnp.where(lane == row, low, 0.0), axis=1, keepdims=True)
    wide = jnp.concatenate([b22, jnp.zeros((REST, MAIN - REST), jnp.float32)], axis=1)
    lane8, row8 = iota((8, MAIN), 1), iota((8, MAIN), 0)
    corner = wide[:8]
    for m in range(1, 4):
        corner = jnp.where(lane8 // REST == m, pltpu.roll(wide[8 * m : 8 * m + 8], REST * m, 1), corner)
    for g in range(8):
        corner = jnp.where(lane8 == HALF + g, diagonal[8 * g : 8 * g + 8], corner)
    corner = jnp.where(lane8 == TRACE_LANE, jnp.where(row8 == 0, trace, 0.0), corner)
    return first, b21, corner


def unpack(packed):
    first, b21, corner = packed[:HALF], packed[HALF : HALF + REST], packed[HALF + REST :]
    turned = first.T
    lane, row = iota((HALF, HALF), 1), iota((HALF, HALF), 0)
    a, at = first[:, :HALF], turned[:HALF]
    diagonal = jnp.concatenate([corner[:, HALF + g : HALF + g + 1] for g in range(8)], axis=0)
    p = jnp.where(lane >= row, a, at)
    r = jnp.where(lane < row, a, jnp.where(lane == row, diagonal, at))
    b11 = jnp.concatenate(
        [
            jnp.concatenate([p, first[:, HALF:]], axis=1),
            jnp.concatenate([turned[HALF:], r], axis=1),
        ],
        axis=0,
    )
    b22 = jnp.concatenate([corner[:, REST * m : REST * m + REST] for m in range(4)], axis=0)
    lane, row = iota((REST, REST), 1), iota((REST, REST), 0)
    b22 = jnp.where((row >= REST // 2) & (lane < REST // 2), b22.T, b22)
    return b11, b21, b22


def block_statistics(act_ref, index, scale):
    piece = act_ref[:, index * BLK : (index + 1) * BLK]
    return dot(piece, piece, 0, 0) * scale


def partial_trace(act_ref, scale):
    x = act_ref[...].astype(jnp.float32)
    return jnp.sum(x * x) * scale


def write(ref, at, parts):
    ref[at, 0:HALF] = parts[0]
    ref[at, HALF : HALF + REST] = parts[1]
    ref[at, HALF + REST : ROWS] = parts[2]


def pack_whole(s, trace):
    return pack(s[:MAIN, :MAIN], s[MAIN:, :MAIN], s[MAIN:, MAIN:], trace)


def statistics_kernel(scale, at_ref, act_ref, keep_ref, send_ref):
    z, y = at_ref[0], at_ref[1]
    trace = partial_trace(act_ref, scale)

    def emit(part, ref):
        for j in range(GROUP):
            s = block_statistics(act_ref, part * GROUP + j, scale)
            write(ref, jnp.bitwise_xor(z, j), pack_whole(s, trace))

    for mine in range(2):

        @pl.when(y == mine)
        def _():
            emit(mine, keep_ref)
            emit(1 - mine, send_ref)


def statistics_plain_kernel(scale, act_ref, out_ref):
    trace = partial_trace(act_ref, scale)
    for j in range(out_ref.shape[0]):
        write(out_ref, j, pack_whole(block_statistics(act_ref, j, scale), trace))


def eliminate(tiles, count):
    lane, sub = iota((8, MAIN), 1), iota((8, MAIN), 0)

    def spread(x):
        return jnp.broadcast_to(x, (8, MAIN))

    for r in range(count // 8):
        k = 8 * r
        t = tiles[r]
        inside = (lane >= k) & (lane < k + 8)
        rows = [
            jnp.where(inside, jnp.where(lane == k + i, 1.0, 0.0), spread(t[i : i + 1, :]))
            for i in range(8)
        ]
        small = [[spread(t[i : i + 1, k + j : k + j + 1]) for j in range(8)] for i in range(8)]
        for a in range(8):
            pivot = 1.0 / small[a][a]
            rows[a] = rows[a] * pivot
            for b in range(a + 1, 8):
                small[a][b] = small[a][b] * pivot
            for c in range(8):
                if c != a:
                    factor = small[c][a]
                    rows[c] = rows[c] - factor * rows[a]
                    for b in range(a + 1, 8):
                        small[c][b] = small[c][b] - factor * small[a][b]
        rows = [jnp.where(inside, -x, x) for x in rows]
        for j in range(len(tiles)):
            total = None
            for i in range(8):
                if j == r:
                    column = jnp.where(sub == i, -1.0, 0.0)
                else:
                    column = spread(tiles[j][:, k + i : k + i + 1])
                total = column * rows[i] if total is None else total + column * rows[i]
            tiles[j] = -total if j == r else jnp.where(inside, 0.0, tiles[j]) - total
    return tiles


def invert(packed, level):
    b11, b21, b22 = unpack(packed)
    lane, row = iota((MAIN, MAIN), 1), iota((MAIN, MAIN), 0)
    b11 = jnp.where(lane == row, b11 + level, b11)
    tiles = [b11[8 * r : 8 * r + 8] for r in range(MAIN // 8)]
    tiles += [b21[8 * r : 8 * r + 8] for r in range(REST // 8)]
    tiles = eliminate(tiles, MAIN)
    inner = jnp.concatenate(tiles[: MAIN // 8], axis=0)
    ratio = jnp.concatenate(tiles[MAIN // 8 :], axis=0)
    lane, row = iota((REST, REST), 1), iota((REST, REST), 0)
    schur = jnp.where(lane == row, b22 + level, b22) - dot(ratio, b21, 1, 1, HIGHEST)
    schur = jnp.concatenate([schur, jnp.zeros((REST, MAIN - REST), jnp.float32)], axis=1)
    last = eliminate([schur[8 * r : 8 * r + 8] for r in range(REST // 8)], REST)
    last = -jnp.concatenate(last, axis=0)[:, :REST]
    side = dot(last, ratio, 1, 0, HIGHEST)
    return pack(dot(ratio, side, 0, 0, HIGHEST) - inner, -side, last, 0.0)


def damping(total):
    return 0.5 * total / D + 1e-06


def invert_kernel(own_ref, a_ref, b_ref, out_ref):
    trace = a_ref[0:1, TRACE_LANE : TRACE_LANE + 1] + b_ref[0:1, TRACE_LANE : TRACE_LANE + 1]
    write(out_ref, 0, invert(own_ref[...], damping(trace)))


def invert_plain_kernel(total_ref, in_ref, out_ref):
    write(out_ref, 0, invert(in_ref[0], damping(total_ref[0])))


def build_weights(packed_ref, first, z, top_ref, mid_ref, end_ref):
    top_ref[...] = jnp.zeros_like(top_ref)
    mid_ref[...] = jnp.zeros_like(mid_ref)
    end_ref[...] = jnp.zeros_like(end_ref)
    for s in range(GROUP):
        b11, b21, b22 = unpack(packed_ref[first + jnp.bitwise_xor(z, s)])
        whole = jnp.concatenate(
            [jnp.concatenate([b11, b21.T], axis=1), jnp.concatenate([b21, b22], axis=1)], axis=0
        )
        high = whole.astype(jnp.bfloat16)
        low = (whole - high.astype(jnp.float32)).astype(jnp.bfloat16)
        lo = s * BLK
        if s < 2:
            cut = min(256 - lo, BLK)
            top_ref[lo : lo + BLK, lo : lo + cut] = high[:, :cut]
            top_ref[384 + lo : 384 + lo + BLK, lo : lo + cut] = low[:, :cut]
        if s == 1:
            mid_ref[lo - 128 : lo - 128 + BLK, 0 : lo + BLK - 256] = high[:, 256 - lo :]
            mid_ref[384 + lo : 384 + lo + BLK, 0 : lo + BLK - 256] = low[:, 256 - lo :]
        if s == 2:
            mid_ref[lo - 128 : lo - 128 + BLK, lo - 256 : lo - 256 + BLK] = high
            mid_ref[384 + lo : 384 + lo + BLK, lo - 256 : lo - 256 + BLK] = low
        if s == 3:
            mid_ref[lo - 128 : lo - 128 + BLK, lo - 256 : 256] = high[:, :32]
            mid_ref[384 + lo : 384 + lo + BLK, lo - 256 : 256] = low[:, :32]
            end_ref[lo - 384 : lo - 384 + BLK, 0:128] = high[:, 32:]
            end_ref[lo - 384 : lo - 384 + BLK, 128:256] = low[:, 32:]


def apply_kernel(n_groups, at_ref, *refs):
    packed = refs[:n_groups]
    grad_ref = refs[n_groups]
    out_ref, top_ref, mid_ref, end_ref = refs[-4:]
    z, live, start = at_ref[0], at_ref[1], at_ref[2]
    which, tile = pl.program_id(0), pl.program_id(1)
    for g in range(n_groups):

        @pl.when((tile == 0) & (which == g))
        def _():
            build_weights(packed[g], 0, z, top_ref, mid_ref, end_ref)

    x = grad_ref[...]
    left, right = x[:, :384], x[:, 128:]
    rows = x.shape[0]
    within = start + tile * rows + iota((rows, 1), 0)
    keep = within < live
    a = dot(jnp.concatenate([left, left], axis=1), top_ref[...], 1, 0)
    out_ref[:, 0:256] = jnp.where(keep, a, 0.0)
    b = dot(jnp.concatenate([right, right], axis=1), mid_ref[...], 1, 0)
    out_ref[:, 256:512] = jnp.where(keep, b, 0.0)
    c = dot(x[:, 384:], end_ref[...], 1, 0)
    out_ref[:, 512:640] = jnp.where(keep, c[:, :128] + c[:, 128:], 0.0)


def row_tile(rows):
    for parts in range(1, rows + 1):
        if rows % parts == 0 and rows // parts <= 432 and (rows // parts) % 16 == 0:
            return rows // parts
    return rows


def apply(groups, columns, grad_rows, z, live, start, before):
    rows = grad_rows.shape[0]
    tile = row_tile(rows)
    n = len(groups)
    at = jnp.stack([z, live, start, *columns]).astype(jnp.int32)

    def column(g, t, at_ref):
        return (t, at_ref[3 + g])

    spec = pl.BlockSpec((tile, WIDE), column)
    ins = [pl.BlockSpec((GROUP, ROWS, MAIN), lambda g, t, at_ref: (0, 0, 0))] * n + [spec]
    args = [*groups, grad_rows]
    aliases = {}
    if before is not None:
        ins.append(pl.BlockSpec(memory_space=pl.ANY))
        args.append(before)
        aliases = {1 + n + 1: 0}
    return pl.pallas_call(
        functools.partial(apply_kernel, n),
        out_shape=jax.ShapeDtypeStruct((rows, D), jnp.float32),
        grid_spec=pltpu.PrefetchScalarGridSpec(
            num_scalar_prefetch=1,
            grid=(n, rows // tile),
            in_specs=ins,
            out_specs=spec,
            scratch_shapes=[
                pltpu.VMEM((768, 256), jnp.bfloat16),
                pltpu.VMEM((1024, 256), jnp.bfloat16),
                pltpu.VMEM((256, 256), jnp.bfloat16),
            ],
        ),
        input_output_aliases=aliases,
        cost_estimate=pl.CostEstimate(
            flops=4 * rows * WIDE * 256 * n, bytes_accessed=6 * rows * WIDE * n, transcendentals=0
        ),
        name="apply",
    )(at, *args)


def swap(x, axis, mask):
    size = lax.axis_size(axis)
    return lax.ppermute(x, axis, [(i, i ^ mask) for i in range(size)])


def shards_small(activations, grad_rows, live_rows):
    scale = 1.0 / (activations.shape[0] * lax.axis_size("dp"))
    i, g = lax.axis_index("dp"), lax.axis_index("grad")
    z, y = i // 2, i % 2
    four = jax.ShapeDtypeStruct((GROUP, ROWS, MAIN), jnp.float32)
    keep, send = pl.pallas_call(
        functools.partial(statistics_kernel, scale),
        out_shape=(four, four),
        in_specs=[SMEM, VMEM],
        out_specs=(VMEM, VMEM),
        name="statistics",
    )(jnp.stack([z, y]).astype(jnp.int32), activations)
    half = keep + swap(send, "dp", 1)
    own = half[0] + swap(half[1], "dp", 2) + swap(half[2], "dp", 4) + swap(half[3], "dp", 6)
    mark = own[HALF + REST :]
    mark = mark + swap(mark, "grad", 2)
    inverse = pl.pallas_call(
        invert_kernel,
        out_shape=jax.ShapeDtypeStruct((1, ROWS, MAIN), jnp.float32),
        in_specs=[VMEM] * 3,
        out_specs=VMEM,
        name="invert",
    )(own, mark, swap(mark, "grad", 1))
    mine = jnp.concatenate([inverse] + [swap(inverse, "dp", d) for d in (2, 4, 6)], axis=0)
    by_y, by_x, by_core = swap(mine, "dp", 1), swap(mine, "grad", 2), swap(mine, "grad", 1)
    by_xy = swap(by_y, "grad", 2)
    by_y_core, by_x_core = swap(by_y, "grad", 1), swap(by_x, "grad", 1)
    by_xy_core = swap(by_xy, "grad", 1)
    live = live_rows[0]
    start = i * grad_rows.shape[0]

    def column(dg, dy):
        return (g ^ dg) * 2 + (y ^ dy)

    out = apply([mine, by_core], [column(0, 0), column(1, 0)], grad_rows, z, live, start, None)
    out = apply(
        [by_y, by_x, by_y_core, by_x_core],
        [column(0, 1), column(2, 0), column(1, 1), column(3, 0)],
        grad_rows, z, live, start, out,
    )
    return apply([by_xy, by_xy_core], [column(2, 1), column(3, 1)], grad_rows, z, live, start, out)


def shards_any(activations, grad_rows, live_rows):
    scale = 1.0 / (activations.shape[0] * lax.axis_size("dp"))
    col_blocks = activations.shape[1] // BLK
    part = pl.pallas_call(
        functools.partial(statistics_plain_kernel, scale),
        out_shape=jax.ShapeDtypeStruct((col_blocks, ROWS, MAIN), jnp.float32),
        in_specs=[VMEM],
        out_specs=VMEM,
        name="statistics",
    )(activations)
    packed = lax.psum(part, "dp")
    total = lax.psum(packed[0, HALF + REST, TRACE_LANE].reshape(1), "grad")
    block = pl.BlockSpec((1, ROWS, MAIN), lambda b: (b, 0, 0))
    owned = pl.pallas_call(
        invert_plain_kernel,
        out_shape=jax.ShapeDtypeStruct((col_blocks, ROWS, MAIN), jnp.float32),
        grid=(col_blocks,),
        in_specs=[SMEM, block],
        out_specs=block,
        name="invert",
    )(total, packed)
    inverses = lax.all_gather(owned, "grad", axis=0, tiled=True)
    n = D // WIDE
    groups = [inverses[GROUP * j : GROUP * j + GROUP] for j in range(n)]
    start = lax.axis_index("dp") * grad_rows.shape[0]
    return apply(
        groups, [jnp.int32(j) for j in range(n)], grad_rows, jnp.int32(0), live_rows[0], start, None
    )


def solution(mesh):
    placed = (P("dp", "grad"), P(("grad", "dp"), None), P("grad"))
    small = mesh.shape["dp"] == 8 and mesh.shape["grad"] == 4
    return jax.shard_map(
        shards_small if small else shards_any,
        mesh=mesh, in_specs=placed, out_specs=P(("grad", "dp"), None), check_vma=False,
    )
```

```python
import functools

import jax
import jax.numpy as jnp
from jax import lax
from jax.experimental import pallas as pl
from jax.experimental.pallas import tpu as pltpu
from jax.sharding import PartitionSpec as P

D = 5120
BLK = 160
MAIN = 128
REST = BLK - MAIN
HALF = 64
ROWS = 104
GROUP = 4
WIDE = GROUP * BLK
TRACE_LANE = 72
VMEM = pl.BlockSpec(memory_space=pltpu.VMEM)
ANY = pl.BlockSpec(memory_space=pl.ANY)
SMEM = pl.BlockSpec(memory_space=pltpu.SMEM)
SCOPED = 52 << 20
SMALL = pltpu.CompilerParams(vmem_limit_bytes=16 << 20)
HIGHEST = lax.Precision.HIGHEST


def iota(shape, dim):
    return lax.broadcasted_iota(jnp.int32, shape, dim)


def dot(a, b, ca, cb, precision=None):
    return lax.dot_general(
        a, b, (((ca,), (cb,)), ((), ())), precision=precision, preferred_element_type=jnp.float32
    )


def pack(b11, b21, b22, trace):
    top, low = b11[:HALF], pltpu.roll(b11[HALF:], HALF, 1)
    lane, row = iota((HALF, MAIN), 1), iota((HALF, MAIN), 0)
    first = jnp.where(lane < row, low, top)
    first = jnp.where(lane < HALF, first, top)
    diagonal = jnp.sum(jnp.where(lane == row, low, 0.0), axis=1, keepdims=True)
    wide = jnp.concatenate([b22, jnp.zeros((REST, MAIN - REST), jnp.float32)], axis=1)
    lane8, row8 = iota((8, MAIN), 1), iota((8, MAIN), 0)
    corner = wide[:8]
    for m in range(1, 4):
        corner = jnp.where(lane8 // REST == m, pltpu.roll(wide[8 * m : 8 * m + 8], REST * m, 1), corner)
    for g in range(8):
        corner = jnp.where(lane8 == HALF + g, diagonal[8 * g : 8 * g + 8], corner)
    corner = jnp.where(lane8 == TRACE_LANE, jnp.where(row8 == 0, trace, 0.0), corner)
    return first, b21, corner


def unpack(packed):
    first, b21, corner = packed[:HALF], packed[HALF : HALF + REST], packed[HALF + REST :]
    turned = first.T
    lane, row = iota((HALF, HALF), 1), iota((HALF, HALF), 0)
    a, at = first[:, :HALF], turned[:HALF]
    diagonal = jnp.concatenate([corner[:, HALF + g : HALF + g + 1] for g in range(8)], axis=0)
    p = jnp.where(lane >= row, a, at)
    r = jnp.where(lane < row, a, jnp.where(lane == row, diagonal, at))
    b11 = jnp.concatenate(
        [
            jnp.concatenate([p, first[:, HALF:]], axis=1),
            jnp.concatenate([turned[HALF:], r], axis=1),
        ],
        axis=0,
    )
    b22 = jnp.concatenate([corner[:, REST * m : REST * m + REST] for m in range(4)], axis=0)
    lane, row = iota((REST, REST), 1), iota((REST, REST), 0)
    b22 = jnp.where((row >= REST // 2) & (lane < REST // 2), b22.T, b22)
    return b11, b21, b22


def block_statistics(act_ref, index, scale):
    piece = act_ref[:, index * BLK : (index + 1) * BLK]
    return dot(piece, piece, 0, 0) * scale


def partial_trace(act_ref, scale):
    x = act_ref[...].astype(jnp.float32)
    return jnp.sum(x * x) * scale


def write(ref, at, parts):
    ref[at, 0:HALF] = parts[0]
    ref[at, HALF : HALF + REST] = parts[1]
    ref[at, HALF + REST : ROWS] = parts[2]


def pack_whole(s, trace):
    return pack(s[:MAIN, :MAIN], s[MAIN:, :MAIN], s[MAIN:, MAIN:], trace)


def send_kernel(scale, act_ref, send_ref, trace_ref):
    i = lax.axis_index("dp")
    z, y = i // 2, i % 2
    emit(act_ref, 1 - y, z, scale, send_ref)
    marked = (iota((8, MAIN), 0) == 0) & (iota((8, MAIN), 1) == TRACE_LANE)
    trace_ref[...] = jnp.where(marked, partial_trace(act_ref, scale), 0.0)


def keep_kernel(scale, act_ref, keep_ref):
    i = lax.axis_index("dp")
    emit(act_ref, i % 2, i // 2, scale, keep_ref)


def emit(act_ref, part, z, scale, ref):
    columns = pl.ds(pl.multiple_of(part * WIDE, MAIN), WIDE)
    half = act_ref[:, columns]
    for j in range(GROUP):
        piece = half[:, j * BLK : (j + 1) * BLK]
        write(ref, jnp.bitwise_xor(z, j), pack_whole(dot(piece, piece, 0, 0) * scale, 0.0))


def statistics_plain_kernel(scale, act_ref, out_ref):
    trace = partial_trace(act_ref, scale)
    for j in range(out_ref.shape[0]):
        write(out_ref, j, pack_whole(block_statistics(act_ref, j, scale), trace))


def eliminate(tiles, count):
    lane, sub = iota((8, MAIN), 1), iota((8, MAIN), 0)

    def spread(x):
        return jnp.broadcast_to(x, (8, MAIN))

    for r in range(count // 8):
        k = 8 * r
        t = tiles[r]
        inside = (lane >= k) & (lane < k + 8)
        rows = [
            jnp.where(inside, jnp.where(lane == k + i, 1.0, 0.0), spread(t[i : i + 1, :]))
            for i in range(8)
        ]
        small = [[spread(t[i : i + 1, k + j : k + j + 1]) for j in range(8)] for i in range(8)]
        for a in range(8):
            pivot = 1.0 / small[a][a]
            rows[a] = rows[a] * pivot
            for b in range(a + 1, 8):
                small[a][b] = small[a][b] * pivot
            for c in range(8):
                if c != a:
                    factor = small[c][a]
                    rows[c] = rows[c] - factor * rows[a]
                    for b in range(a + 1, 8):
                        small[c][b] = small[c][b] - factor * small[a][b]
        rows = [jnp.where(inside, -x, x) for x in rows]
        for j in range(len(tiles)):
            total = None
            for i in range(8):
                if j == r:
                    column = jnp.where(sub == i, -1.0, 0.0)
                else:
                    column = spread(tiles[j][:, k + i : k + i + 1])
                total = column * rows[i] if total is None else total + column * rows[i]
            tiles[j] = -total if j == r else jnp.where(inside, 0.0, tiles[j]) - total
    return tiles


def invert(packed, level):
    b11, b21, b22 = unpack(packed)
    lane, row = iota((MAIN, MAIN), 1), iota((MAIN, MAIN), 0)
    b11 = jnp.where(lane == row, b11 + level, b11)
    tiles = [b11[8 * r : 8 * r + 8] for r in range(MAIN // 8)]
    tiles += [b21[8 * r : 8 * r + 8] for r in range(REST // 8)]
    tiles = eliminate(tiles, MAIN)
    inner = jnp.concatenate(tiles[: MAIN // 8], axis=0)
    ratio = jnp.concatenate(tiles[MAIN // 8 :], axis=0)
    lane, row = iota((REST, REST), 1), iota((REST, REST), 0)
    schur = jnp.where(lane == row, b22 + level, b22) - dot(ratio, b21, 1, 1, HIGHEST)
    schur = jnp.concatenate([schur, jnp.zeros((REST, MAIN - REST), jnp.float32)], axis=1)
    last = eliminate([schur[8 * r : 8 * r + 8] for r in range(REST // 8)], REST)
    last = -jnp.concatenate(last, axis=0)[:, :REST]
    side = dot(last, ratio, 1, 0, HIGHEST)
    return pack(dot(ratio, side, 0, 0, HIGHEST) - inner, -side, last, 0.0)


def damping(total):
    return 0.5 * total / D + 1e-06


def invert_kernel(a_ref, b_ref, c_ref, d_ref, out_ref):
    own = a_ref[0] + b_ref[0] + c_ref[0] + d_ref[0]
    trace = own[HALF + REST : HALF + REST + 1, TRACE_LANE : TRACE_LANE + 1]
    write(out_ref, 0, invert(own, damping(trace)))


def invert_plain_kernel(total_ref, in_ref, out_ref):
    write(out_ref, 0, invert(in_ref[0], damping(total_ref[0])))


def build_weights(packed_ref, z, top_ref, mid_ref, end_ref):
    top_ref[...] = jnp.zeros_like(top_ref)
    mid_ref[...] = jnp.zeros_like(mid_ref)
    end_ref[...] = jnp.zeros_like(end_ref)
    for s in range(GROUP):
        b11, b21, b22 = unpack(packed_ref[jnp.bitwise_xor(z, s)])
        whole = jnp.concatenate(
            [jnp.concatenate([b11, b21.T], axis=1), jnp.concatenate([b21, b22], axis=1)], axis=0
        )
        high = whole.astype(jnp.bfloat16)
        low = (whole - high.astype(jnp.float32)).astype(jnp.bfloat16)
        lo = s * BLK
        if s < 2:
            cut = min(256 - lo, BLK)
            top_ref[lo : lo + BLK, lo : lo + cut] = high[:, :cut]
            top_ref[384 + lo : 384 + lo + BLK, lo : lo + cut] = low[:, :cut]
        if s == 1:
            mid_ref[lo - 128 : lo - 128 + BLK, 0 : lo + BLK - 256] = high[:, 256 - lo :]
            mid_ref[384 + lo : 384 + lo + BLK, 0 : lo + BLK - 256] = low[:, 256 - lo :]
        if s == 2:
            mid_ref[lo - 128 : lo - 128 + BLK, lo - 256 : lo - 256 + BLK] = high
            mid_ref[384 + lo : 384 + lo + BLK, lo - 256 : lo - 256 + BLK] = low
        if s == 3:
            mid_ref[lo - 128 : lo - 128 + BLK, lo - 256 : 256] = high[:, :32]
            mid_ref[384 + lo : 384 + lo + BLK, lo - 256 : 256] = low[:, :32]
            end_ref[lo - 384 : lo - 384 + BLK, 0:128] = high[:, 32:]
            end_ref[lo - 384 : lo - 384 + BLK, 128:256] = low[:, 32:]


def apply_kernel(first, n_groups, at_ref, *refs):
    packed, grad_ref = refs[:n_groups], refs[n_groups]
    out_ref, *weights, buffer, sems, piece, piece_sems = refs[-11:]
    z, live, start = at_ref[0], at_ref[1], at_ref[2]
    rows = grad_ref.shape[0]
    parts = 3 if rows % 48 == 0 else 1
    keep = start + iota((rows, 1), 0) < live

    def build(g):
        build_weights(packed[g], z, *weights[3 * (g % 2) : 3 * (g % 2) + 3])

    def copy(g, tile):
        lo, width = 256 * tile, min(256, WIDE - 256 * tile)
        column = pl.multiple_of(at_ref[3 + first + g] * WIDE + lo, MAIN)
        return pltpu.make_async_copy(
            buffer.at[g % 2, :, lo : lo + width],
            out_ref.at[:, pl.ds(column, width)],
            sems.at[g % 2, tile],
        )

    def fetch(g):
        column = pl.multiple_of(at_ref[3 + first + g] * WIDE, MAIN)
        return pltpu.make_async_copy(
            grad_ref.at[:, pl.ds(column, WIDE)], piece.at[g], piece_sems.at[g]
        )

    def multiply(g):
        top_ref, mid_ref, end_ref = weights[3 * (g % 2) : 3 * (g % 2) + 3]
        for part in range(parts):
            here = slice(part * rows // parts, (part + 1) * rows // parts)
            x, kept = piece[g, here], keep[here]
            left, right = x[:, :384], x[:, 128:]
            a = dot(jnp.concatenate([left, left], axis=1), top_ref[...], 1, 0)
            buffer[g % 2, here, 0:256] = jnp.where(kept, a, 0.0)
        copy(g, 0).start()
        if g + 1 < n_groups:
            build(g + 1)
        for part in range(parts):
            here = slice(part * rows // parts, (part + 1) * rows // parts)
            x, kept = piece[g, here], keep[here]
            left, right = x[:, :384], x[:, 128:]
            b = dot(jnp.concatenate([right, right], axis=1), mid_ref[...], 1, 0)
            buffer[g % 2, here, 256:512] = jnp.where(kept, b, 0.0)
            c = dot(x[:, 384:], end_ref[...], 1, 0)
            buffer[g % 2, here, 512:640] = jnp.where(kept, c[:, :128] + c[:, 128:], 0.0)
        copy(g, 1).start()
        copy(g, 2).start()

    for g in range(n_groups):
        fetch(g).start()
    build(0)
    for g in range(n_groups):
        if g >= 2:
            for tile in range(3):
                copy(g - 2, tile).wait()
        fetch(g).wait()
        pl.when(start >= 0)(functools.partial(multiply, g))
    for g in range(max(0, n_groups - 2), n_groups):
        for tile in range(3):
            copy(g, tile).wait()


def apply(groups, first, at, grad_rows, before):
    rows = grad_rows.shape[0]
    n = len(groups)
    args = [*groups, grad_rows]
    ins = [SMEM] + [VMEM] * n + [ANY]
    aliases = {}
    if before is not None:
        ins.append(ANY)
        args.append(before)
        aliases = {1 + n + 1: 0}
    return pl.pallas_call(
        functools.partial(apply_kernel, first, n),
        out_shape=jax.ShapeDtypeStruct((rows, D), jnp.float32),
        in_specs=ins,
        out_specs=ANY,
        scratch_shapes=[pltpu.VMEM((k, 256), jnp.bfloat16) for k in (768, 1024, 256)] * 2
        + [pltpu.VMEM((2, rows, WIDE), jnp.float32), pltpu.SemaphoreType.DMA((2, 3))]
        + [pltpu.VMEM((n, rows, WIDE), jnp.bfloat16), pltpu.SemaphoreType.DMA((n,))],
        input_output_aliases=aliases,
        compiler_params=pltpu.CompilerParams(vmem_limit_bytes=SCOPED),
        cost_estimate=pl.CostEstimate(
            flops=4 * rows * WIDE * 256 * n, bytes_accessed=4 * rows * WIDE * n, transcendentals=0
        ),
        name="apply",
    )(at, *args)


def swap(x, axis, mask):
    size = lax.axis_size(axis)
    return lax.ppermute(x, axis, [(i, i ^ mask) for i in range(size)])


def shards_small(activations, grad_rows, live_rows):
    scale = 1.0 / (activations.shape[0] * lax.axis_size("dp"))
    i, g = lax.axis_index("dp"), lax.axis_index("grad")
    z, y = i // 2, i % 2
    four = jax.ShapeDtypeStruct((GROUP, ROWS, MAIN), jnp.float32)
    send, trace = pl.pallas_call(
        functools.partial(send_kernel, scale),
        out_shape=(four, jax.ShapeDtypeStruct((8, MAIN), jnp.float32)),
        in_specs=[VMEM],
        out_specs=(VMEM, VMEM),
        compiler_params=SMALL,
        name="statistics_send",
    )(activations)
    received = swap(send, "dp", 1)
    keep = pl.pallas_call(
        functools.partial(keep_kernel, scale),
        out_shape=four,
        in_specs=[VMEM],
        out_specs=VMEM,
        compiler_params=SMALL,
        name="statistics_keep",
    )(activations)
    trace = trace + swap(trace, "grad", 1)
    trace = trace + swap(trace, "grad", 2)
    trace = trace + swap(trace, "dp", 1)
    half = keep + received
    half = half.at[:, HALF + REST :].add(trace[None])
    inverse = pl.pallas_call(
        invert_kernel,
        out_shape=jax.ShapeDtypeStruct((1, ROWS, MAIN), jnp.float32),
        in_specs=[VMEM] * 4,
        out_specs=VMEM,
        compiler_params=SMALL,
        name="invert",
    )(half[0:1], *[swap(half[e : e + 1], "dp", 2 * e) for e in range(1, 4)])
    mine = jnp.concatenate([inverse] + [swap(inverse, "dp", d) for d in (2, 4, 6)], axis=0)
    by_y, by_x, by_core = swap(mine, "dp", 1), swap(mine, "grad", 2), swap(mine, "grad", 1)
    by_xy = swap(by_y, "grad", 2)
    by_y_core, by_x_core = swap(by_y, "grad", 1), swap(by_x, "grad", 1)
    by_xy_core = swap(by_xy, "grad", 1)
    order = ((0, 0), (1, 0), (0, 1), (2, 0), (1, 1), (3, 0), (2, 1), (3, 1))
    columns = [(g ^ dg) * 2 + (y ^ dy) for dg, dy in order]
    at = jnp.stack([z, live_rows[0], i * grad_rows.shape[0], *columns]).astype(jnp.int32)
    out = apply([mine, by_core], 0, at, grad_rows, None)
    out = apply([by_y, by_x, by_y_core, by_x_core], 2, at, grad_rows, out)
    return apply([by_xy, by_xy_core], 6, at, grad_rows, out)


def shards_any(activations, grad_rows, live_rows):
    scale = 1.0 / (activations.shape[0] * lax.axis_size("dp"))
    col_blocks = activations.shape[1] // BLK
    part = pl.pallas_call(
        functools.partial(statistics_plain_kernel, scale),
        out_shape=jax.ShapeDtypeStruct((col_blocks, ROWS, MAIN), jnp.float32),
        in_specs=[VMEM],
        out_specs=VMEM,
        name="statistics",
    )(activations)
    packed = lax.psum(part, "dp")
    total = lax.psum(packed[0, HALF + REST, TRACE_LANE].reshape(1), "grad")
    block = pl.BlockSpec((1, ROWS, MAIN), lambda b: (b, 0, 0))
    owned = pl.pallas_call(
        invert_plain_kernel,
        out_shape=jax.ShapeDtypeStruct((col_blocks, ROWS, MAIN), jnp.float32),
        grid=(col_blocks,),
        in_specs=[SMEM, block],
        out_specs=block,
        name="invert",
    )(total, packed)
    inverses = lax.all_gather(owned, "grad", axis=0, tiled=True)
    n = D // WIDE
    groups = [inverses[GROUP * j : GROUP * j + GROUP] for j in range(n)]
    start = lax.axis_index("dp") * grad_rows.shape[0]
    at = jnp.stack([jnp.int32(0), live_rows[0], start, *range(n)]).astype(jnp.int32)
    return apply(groups, 0, at, grad_rows, None)


def solution(mesh):
    placed = (P("dp", "grad"), P(("grad", "dp"), None), P("grad"))
    small = mesh.shape["dp"] == 8 and mesh.shape["grad"] == 4
    return jax.shard_map(
        shards_small if small else shards_any,
        mesh=mesh, in_specs=placed, out_specs=P(("grad", "dp"), None), check_vma=False,
    )
```

```python
import functools

import jax
import jax.numpy as jnp
from jax import lax
from jax.experimental import pallas as pl
from jax.experimental.pallas import tpu as pltpu
from jax.sharding import PartitionSpec as P

D = 5120
BLK = 160
MAIN = 128
REST = BLK - MAIN
HALF = 64
ROWS = 104
GROUP = 4
WIDE = GROUP * BLK
TRACE_LANE = 72
VMEM = pl.BlockSpec(memory_space=pltpu.VMEM)
ANY = pl.BlockSpec(memory_space=pl.ANY)
SMEM = pl.BlockSpec(memory_space=pltpu.SMEM)
SCOPED = 52 << 20
SMALL = pltpu.CompilerParams(vmem_limit_bytes=16 << 20)
HIGHEST = lax.Precision.HIGHEST


def iota(shape, dim):
    return lax.broadcasted_iota(jnp.int32, shape, dim)


def dot(a, b, ca, cb, precision=None):
    return lax.dot_general(
        a, b, (((ca,), (cb,)), ((), ())), precision=precision, preferred_element_type=jnp.float32
    )


def pack(b11, b21, b22, trace):
    top, low = b11[:HALF], pltpu.roll(b11[HALF:], HALF, 1)
    lane, row = iota((HALF, MAIN), 1), iota((HALF, MAIN), 0)
    first = jnp.where(lane < row, low, top)
    first = jnp.where(lane < HALF, first, top)
    diagonal = jnp.sum(jnp.where(lane == row, low, 0.0), axis=1, keepdims=True)
    wide = jnp.concatenate([b22, jnp.zeros((REST, MAIN - REST), jnp.float32)], axis=1)
    lane8, row8 = iota((8, MAIN), 1), iota((8, MAIN), 0)
    corner = wide[:8]
    for m in range(1, 4):
        corner = jnp.where(lane8 // REST == m, pltpu.roll(wide[8 * m : 8 * m + 8], REST * m, 1), corner)
    for g in range(8):
        corner = jnp.where(lane8 == HALF + g, diagonal[8 * g : 8 * g + 8], corner)
    corner = jnp.where(lane8 == TRACE_LANE, jnp.where(row8 == 0, trace, 0.0), corner)
    return first, b21, corner


def unpack(packed):
    first, b21, corner = packed[:HALF], packed[HALF : HALF + REST], packed[HALF + REST :]
    turned = first.T
    lane, row = iota((HALF, HALF), 1), iota((HALF, HALF), 0)
    a, at = first[:, :HALF], turned[:HALF]
    diagonal = jnp.concatenate([corner[:, HALF + g : HALF + g + 1] for g in range(8)], axis=0)
    p = jnp.where(lane >= row, a, at)
    r = jnp.where(lane < row, a, jnp.where(lane == row, diagonal, at))
    b11 = jnp.concatenate(
        [
            jnp.concatenate([p, first[:, HALF:]], axis=1),
            jnp.concatenate([turned[HALF:], r], axis=1),
        ],
        axis=0,
    )
    b22 = jnp.concatenate([corner[:, REST * m : REST * m + REST] for m in range(4)], axis=0)
    lane, row = iota((REST, REST), 1), iota((REST, REST), 0)
    b22 = jnp.where((row >= REST // 2) & (lane < REST // 2), b22.T, b22)
    return b11, b21, b22


def block_statistics(act_ref, index, scale):
    piece = act_ref[:, index * BLK : (index + 1) * BLK]
    return dot(piece, piece, 0, 0) * scale


def partial_trace(act_ref, scale):
    x = act_ref[...].astype(jnp.float32)
    return jnp.sum(x * x) * scale


def write(ref, at, parts):
    ref[at, 0:HALF] = parts[0]
    ref[at, HALF : HALF + REST] = parts[1]
    ref[at, HALF + REST : ROWS] = parts[2]


def pack_whole(s, trace):
    return pack(s[:MAIN, :MAIN], s[MAIN:, :MAIN], s[MAIN:, MAIN:], trace)


def send_kernel(scale, act_ref, send_ref, trace_ref):
    i = lax.axis_index("dp")
    z, y = i // 2, i % 2
    emit(act_ref, 1 - y, z, scale, send_ref)
    marked = (iota((8, MAIN), 0) == 0) & (iota((8, MAIN), 1) == TRACE_LANE)
    trace_ref[...] = jnp.where(marked, partial_trace(act_ref, scale), 0.0)


def keep_kernel(scale, act_ref, keep_ref):
    i = lax.axis_index("dp")
    emit(act_ref, i % 2, i // 2, scale, keep_ref)


def emit(act_ref, part, z, scale, ref):
    columns = pl.ds(pl.multiple_of(part * WIDE, MAIN), WIDE)
    half = act_ref[:, columns]
    for j in range(GROUP):
        piece = half[:, j * BLK : (j + 1) * BLK]
        write(ref, jnp.bitwise_xor(z, j), pack_whole(dot(piece, piece, 0, 0) * scale, 0.0))


def statistics_plain_kernel(scale, act_ref, out_ref):
    trace = partial_trace(act_ref, scale)
    for j in range(out_ref.shape[0]):
        write(out_ref, j, pack_whole(block_statistics(act_ref, j, scale), trace))


def eliminate(tiles, count):
    lane, sub = iota((8, MAIN), 1), iota((8, MAIN), 0)

    def spread(x):
        return jnp.broadcast_to(x, (8, MAIN))

    for r in range(count // 8):
        k = 8 * r
        t = tiles[r]
        inside = (lane >= k) & (lane < k + 8)
        rows = [
            jnp.where(inside, jnp.where(lane == k + i, 1.0, 0.0), spread(t[i : i + 1, :]))
            for i in range(8)
        ]
        small = [[spread(t[i : i + 1, k + j : k + j + 1]) for j in range(8)] for i in range(8)]
        for a in range(8):
            pivot = 1.0 / small[a][a]
            rows[a] = rows[a] * pivot
            for b in range(a + 1, 8):
                small[a][b] = small[a][b] * pivot
            for c in range(8):
                if c != a:
                    factor = small[c][a]
                    rows[c] = rows[c] - factor * rows[a]
                    for b in range(a + 1, 8):
                        small[c][b] = small[c][b] - factor * small[a][b]
        rows = [jnp.where(inside, -x, x) for x in rows]
        for j in range(len(tiles)):
            total = None
            for i in range(8):
                if j == r:
                    column = jnp.where(sub == i, -1.0, 0.0)
                else:
                    column = spread(tiles[j][:, k + i : k + i + 1])
                total = column * rows[i] if total is None else total + column * rows[i]
            tiles[j] = -total if j == r else jnp.where(inside, 0.0, tiles[j]) - total
    return tiles


def invert(packed, level):
    b11, b21, b22 = unpack(packed)
    lane, row = iota((MAIN, MAIN), 1), iota((MAIN, MAIN), 0)
    b11 = jnp.where(lane == row, b11 + level, b11)
    tiles = [b11[8 * r : 8 * r + 8] for r in range(MAIN // 8)]
    tiles += [b21[8 * r : 8 * r + 8] for r in range(REST // 8)]
    tiles = eliminate(tiles, MAIN)
    inner = jnp.concatenate(tiles[: MAIN // 8], axis=0)
    ratio = jnp.concatenate(tiles[MAIN // 8 :], axis=0)
    lane, row = iota((REST, REST), 1), iota((REST, REST), 0)
    schur = jnp.where(lane == row, b22 + level, b22) - dot(ratio, b21, 1, 1, HIGHEST)
    schur = jnp.concatenate([schur, jnp.zeros((REST, MAIN - REST), jnp.float32)], axis=1)
    last = eliminate([schur[8 * r : 8 * r + 8] for r in range(REST // 8)], REST)
    last = -jnp.concatenate(last, axis=0)[:, :REST]
    side = dot(last, ratio, 1, 0, HIGHEST)
    return pack(dot(ratio, side, 0, 0, HIGHEST) - inner, -side, last, 0.0)


def damping(total):
    return 0.5 * total / D + 1e-06


def invert_kernel(a_ref, b_ref, c_ref, d_ref, out_ref):
    own = a_ref[0] + b_ref[0] + c_ref[0] + d_ref[0]
    trace = own[HALF + REST : HALF + REST + 1, TRACE_LANE : TRACE_LANE + 1]
    write(out_ref, 0, invert(own, damping(trace)))


def invert_plain_kernel(total_ref, in_ref, out_ref):
    write(out_ref, 0, invert(in_ref[0], damping(total_ref[0])))


def halves(packed_ref, place):
    b11, b21, b22 = unpack(packed_ref[place])
    whole = jnp.concatenate(
        [jnp.concatenate([b11, b21.T], axis=1), jnp.concatenate([b21, b22], axis=1)], axis=0
    )
    high = whole.astype(jnp.bfloat16)
    return high, (whole - high.astype(jnp.float32)).astype(jnp.bfloat16)


def build_first(packed_ref, z, top_ref, mid_ref):
    top_ref[...] = jnp.zeros_like(top_ref)
    mid_ref[...] = jnp.zeros_like(mid_ref)
    for at, part in zip((0, 384), halves(packed_ref, z)):
        top_ref[at : at + BLK, 0:BLK] = part
    for at, part in zip((0, 384), halves(packed_ref, jnp.bitwise_xor(z, 1))):
        top_ref[at + BLK : at + 2 * BLK, BLK:256] = part[:, : 256 - BLK]
    for at, part in zip((0, 512), halves(packed_ref, jnp.bitwise_xor(z, 1))):
        mid_ref[at + 32 : at + 32 + BLK, 0:64] = part[:, 96:]


def build_rest(packed_ref, z, mid_ref, end_ref):
    end_ref[...] = jnp.zeros_like(end_ref)
    for at, part in zip((0, 512), halves(packed_ref, jnp.bitwise_xor(z, 2))):
        mid_ref[at + 192 : at + 192 + BLK, 64 : 64 + BLK] = part
    for at, part in zip((0, 512), halves(packed_ref, jnp.bitwise_xor(z, 3))):
        mid_ref[at + 352 : at + 352 + BLK, 224:256] = part[:, :32]
        end_ref[96 : 96 + BLK, at // 4 : at // 4 + 128] = part[:, 32:]


def apply_kernel(first, n_groups, at_ref, *refs):
    packed, grad_ref = refs[:n_groups], refs[n_groups]
    out_ref, *weights, buffer, sems, held, held_sems = refs[-11:]
    z, live, start = at_ref[0], at_ref[1], at_ref[2]
    rows = grad_ref.shape[0]
    parts = row_parts(rows)
    keep = start + iota((rows, 1), 0) < live

    def build(g, first_part, last_part):
        top_ref, mid_ref, end_ref = weights[3 * (g % 2) : 3 * (g % 2) + 3]
        if first_part:
            build_first(packed[g], z, top_ref, mid_ref)
        if last_part:
            build_rest(packed[g], z, mid_ref, end_ref)

    def copy(g, tile):
        lo, width = 256 * tile, min(256, WIDE - 256 * tile)
        column = pl.multiple_of(at_ref[3 + first + g] * WIDE + lo, MAIN)
        return pltpu.make_async_copy(
            buffer.at[g % 2, :, lo : lo + width],
            out_ref.at[:, pl.ds(column, width)],
            sems.at[g % 2, tile],
        )

    def fetch(g):
        column = pl.multiple_of(at_ref[3 + first + g] * WIDE, MAIN)
        return pltpu.make_async_copy(grad_ref.at[:, pl.ds(column, WIDE)], held.at[g], held_sems.at[g])

    def multiply(g):
        top_ref, mid_ref, end_ref = weights[3 * (g % 2) : 3 * (g % 2) + 3]
        if g == 0:
            build(0, True, False)
        for part in range(parts):
            here = slice(part * rows // parts, (part + 1) * rows // parts)
            left = held[g, here, 0:384]
            a = dot(jnp.concatenate([left, left], axis=1), top_ref[...], 1, 0)
            buffer[g % 2, here, 0:256] = jnp.where(keep[here], a, 0.0)
        copy(g, 0).start()
        if g == 0:
            build(0, False, True)
        if g + 1 < n_groups:
            build(g + 1, True, True)
        for part in range(parts):
            here = slice(part * rows // parts, (part + 1) * rows // parts)
            kept, right, end = keep[here], held[g, here, 128:640], held[g, here, 384:640]
            b = dot(jnp.concatenate([right, right], axis=1), mid_ref[...], 1, 0)
            buffer[g % 2, here, 256:512] = jnp.where(kept, b, 0.0)
            c = dot(end, end_ref[...], 1, 0)
            buffer[g % 2, here, 512:640] = jnp.where(kept, c[:, :128] + c[:, 128:], 0.0)
        copy(g, 1).start()
        copy(g, 2).start()

    for g in range(n_groups):
        fetch(g).start()
    for g in range(n_groups):
        if g >= 2:
            for tile in range(3):
                copy(g - 2, tile).wait()
        fetch(g).wait()
        pl.when(start >= 0)(functools.partial(multiply, g))
    for g in range(max(0, n_groups - 2), n_groups):
        for tile in range(3):
            copy(g, tile).wait()


def row_parts(rows):
    return 3 if rows % 48 == 0 else 1


def apply(groups, first, at, grad_rows, before):
    rows = grad_rows.shape[0]
    n = len(groups)
    args = [*groups, grad_rows]
    ins = [SMEM] + [VMEM] * n + [ANY]
    aliases = {}
    if before is not None:
        ins.append(ANY)
        args.append(before)
        aliases = {1 + n + 1: 0}
    return pl.pallas_call(
        functools.partial(apply_kernel, first, n),
        out_shape=jax.ShapeDtypeStruct((rows, D), jnp.float32),
        in_specs=ins,
        out_specs=ANY,
        scratch_shapes=[pltpu.VMEM((k, 256), jnp.bfloat16) for k in (768, 1024, 256)] * 2
        + [pltpu.VMEM((2, rows, WIDE), jnp.float32), pltpu.SemaphoreType.DMA((2, 3))]
        + [pltpu.VMEM((n, rows, WIDE), jnp.bfloat16), pltpu.SemaphoreType.DMA((n,))],
        input_output_aliases=aliases,
        compiler_params=pltpu.CompilerParams(vmem_limit_bytes=SCOPED),
        cost_estimate=pl.CostEstimate(
            flops=4 * rows * WIDE * 256 * n, bytes_accessed=4 * rows * WIDE * n, transcendentals=0
        ),
        name="apply",
    )(at, *args)


def swap(x, axis, mask):
    size = lax.axis_size(axis)
    return lax.ppermute(x, axis, [(i, i ^ mask) for i in range(size)])


def shards_small(activations, grad_rows, live_rows):
    scale = 1.0 / (activations.shape[0] * lax.axis_size("dp"))
    i, g = lax.axis_index("dp"), lax.axis_index("grad")
    z, y = i // 2, i % 2
    four = jax.ShapeDtypeStruct((GROUP, ROWS, MAIN), jnp.float32)
    send, trace = pl.pallas_call(
        functools.partial(send_kernel, scale),
        out_shape=(four, jax.ShapeDtypeStruct((8, MAIN), jnp.float32)),
        in_specs=[VMEM],
        out_specs=(VMEM, VMEM),
        compiler_params=SMALL,
        name="statistics_send",
    )(activations)
    received = swap(send, "dp", 1)
    keep = pl.pallas_call(
        functools.partial(keep_kernel, scale),
        out_shape=four,
        in_specs=[VMEM],
        out_specs=VMEM,
        compiler_params=SMALL,
        name="statistics_keep",
    )(activations)
    trace = trace + swap(trace, "grad", 1)
    trace = trace + swap(trace, "grad", 2)
    trace = trace + swap(trace, "dp", 1)
    half = keep + received
    half = half.at[:, HALF + REST :].add(trace[None])
    inverse = pl.pallas_call(
        invert_kernel,
        out_shape=jax.ShapeDtypeStruct((1, ROWS, MAIN), jnp.float32),
        in_specs=[VMEM] * 4,
        out_specs=VMEM,
        compiler_params=SMALL,
        name="invert",
    )(half[0:1], *[swap(half[e : e + 1], "dp", 2 * e) for e in range(1, 4)])
    mine = jnp.concatenate([inverse] + [swap(inverse, "dp", d) for d in (2, 4, 6)], axis=0)
    by_y, by_x, by_core = swap(mine, "dp", 1), swap(mine, "grad", 2), swap(mine, "grad", 1)
    order = ((0, 0), (1, 0), (0, 1), (2, 0), (1, 1), (3, 0), (2, 1), (3, 1))
    columns = [(g ^ dg) * 2 + (y ^ dy) for dg, dy in order]
    at = jnp.stack([z, live_rows[0], i * grad_rows.shape[0], *columns]).astype(jnp.int32)
    out = apply([mine], 0, at, grad_rows, None)
    by_y, out = lax.optimization_barrier((by_y, out))
    by_xy = swap(by_y, "grad", 2)
    by_y_core, by_x_core = swap(by_y, "grad", 1), swap(by_x, "grad", 1)
    out = apply([by_core, by_y, by_x], 1, at, grad_rows, out)
    by_xy, out = lax.optimization_barrier((by_xy, out))
    by_xy_core = swap(by_xy, "grad", 1)
    return apply([by_y_core, by_x_core, by_xy, by_xy_core], 4, at, grad_rows, out)


def shards_any(activations, grad_rows, live_rows):
    scale = 1.0 / (activations.shape[0] * lax.axis_size("dp"))
    col_blocks = activations.shape[1] // BLK
    part = pl.pallas_call(
        functools.partial(statistics_plain_kernel, scale),
        out_shape=jax.ShapeDtypeStruct((col_blocks, ROWS, MAIN), jnp.float32),
        in_specs=[VMEM],
        out_specs=VMEM,
        name="statistics",
    )(activations)
    packed = lax.psum(part, "dp")
    total = lax.psum(packed[0, HALF + REST, TRACE_LANE].reshape(1), "grad")
    block = pl.BlockSpec((1, ROWS, MAIN), lambda b: (b, 0, 0))
    owned = pl.pallas_call(
        invert_plain_kernel,
        out_shape=jax.ShapeDtypeStruct((col_blocks, ROWS, MAIN), jnp.float32),
        grid=(col_blocks,),
        in_specs=[SMEM, block],
        out_specs=block,
        name="invert",
    )(total, packed)
    inverses = lax.all_gather(owned, "grad", axis=0, tiled=True)
    n = D // WIDE
    groups = [inverses[GROUP * j : GROUP * j + GROUP] for j in range(n)]
    start = lax.axis_index("dp") * grad_rows.shape[0]
    at = jnp.stack([jnp.int32(0), live_rows[0], start, *range(n)]).astype(jnp.int32)
    return apply(groups, 0, at, grad_rows, None)


def solution(mesh):
    placed = (P("dp", "grad"), P(("grad", "dp"), None), P("grad"))
    small = mesh.shape["dp"] == 8 and mesh.shape["grad"] == 4
    return jax.shard_map(
        shards_small if small else shards_any,
        mesh=mesh, in_specs=placed, out_specs=P(("grad", "dp"), None), check_vma=False,
    )
```

```python
import functools

import jax
import jax.numpy as jnp
from jax import lax
from jax.experimental import pallas as pl
from jax.experimental.pallas import tpu as pltpu
from jax.sharding import PartitionSpec as P

D = 5120
BLK = 160
MAIN = 128
REST = BLK - MAIN
HALF = 64
ROWS = 104
GROUP = 4
WIDE = GROUP * BLK
TRACE_LANE = 72
VMEM = pl.BlockSpec(memory_space=pltpu.VMEM)
ANY = pl.BlockSpec(memory_space=pl.ANY)
SMEM = pl.BlockSpec(memory_space=pltpu.SMEM)
SMALL = pltpu.CompilerParams(vmem_limit_bytes=16 << 20)
HIGHEST = lax.Precision.HIGHEST


def iota(shape, dim):
    return lax.broadcasted_iota(jnp.int32, shape, dim)


def dot(a, b, ca, cb, precision=None):
    return lax.dot_general(
        a, b, (((ca,), (cb,)), ((), ())), precision=precision, preferred_element_type=jnp.float32
    )


def pack(b11, b21, b22, trace):
    top, low = b11[:HALF], pltpu.roll(b11[HALF:], HALF, 1)
    lane, row = iota((HALF, MAIN), 1), iota((HALF, MAIN), 0)
    first = jnp.where(lane < row, low, top)
    first = jnp.where(lane < HALF, first, top)
    diagonal = jnp.sum(jnp.where(lane == row, low, 0.0), axis=1, keepdims=True)
    wide = jnp.concatenate([b22, jnp.zeros((REST, MAIN - REST), jnp.float32)], axis=1)
    lane8, row8 = iota((8, MAIN), 1), iota((8, MAIN), 0)
    corner = wide[:8]
    for m in range(1, 4):
        corner = jnp.where(lane8 // REST == m, pltpu.roll(wide[8 * m : 8 * m + 8], REST * m, 1), corner)
    for g in range(8):
        corner = jnp.where(lane8 == HALF + g, diagonal[8 * g : 8 * g + 8], corner)
    corner = jnp.where(lane8 == TRACE_LANE, jnp.where(row8 == 0, trace, 0.0), corner)
    return first, b21, corner


def unpack(packed):
    first, b21, corner = packed[:HALF], packed[HALF : HALF + REST], packed[HALF + REST :]
    turned = first.T
    lane, row = iota((HALF, HALF), 1), iota((HALF, HALF), 0)
    a, at = first[:, :HALF], turned[:HALF]
    diagonal = jnp.concatenate([corner[:, HALF + g : HALF + g + 1] for g in range(8)], axis=0)
    p = jnp.where(lane >= row, a, at)
    r = jnp.where(lane < row, a, jnp.where(lane == row, diagonal, at))
    b11 = jnp.concatenate(
        [
            jnp.concatenate([p, first[:, HALF:]], axis=1),
            jnp.concatenate([turned[HALF:], r], axis=1),
        ],
        axis=0,
    )
    b22 = jnp.concatenate([corner[:, REST * m : REST * m + REST] for m in range(4)], axis=0)
    lane, row = iota((REST, REST), 1), iota((REST, REST), 0)
    b22 = jnp.where((row >= REST // 2) & (lane < REST // 2), b22.T, b22)
    return b11, b21, b22


def block_statistics(act_ref, index, scale):
    piece = act_ref[:, index * BLK : (index + 1) * BLK]
    return dot(piece, piece, 0, 0) * scale


def partial_trace(act_ref, scale):
    x = act_ref[...].astype(jnp.float32)
    return jnp.sum(x * x) * scale


def write(ref, at, parts):
    ref[at, 0:HALF] = parts[0]
    ref[at, HALF : HALF + REST] = parts[1]
    ref[at, HALF + REST : ROWS] = parts[2]


def pack_whole(s, trace):
    return pack(s[:MAIN, :MAIN], s[MAIN:, :MAIN], s[MAIN:, MAIN:], trace)


def send_kernel(scale, act_ref, send_ref, trace_ref):
    i = lax.axis_index("dp")
    z, y = i // 2, i % 2
    emit(act_ref, 1 - y, z, scale, send_ref)
    marked = (iota((8, MAIN), 0) == 0) & (iota((8, MAIN), 1) == TRACE_LANE)
    trace_ref[...] = jnp.where(marked, partial_trace(act_ref, scale), 0.0)


def keep_kernel(scale, act_ref, keep_ref):
    i = lax.axis_index("dp")
    emit(act_ref, i % 2, i // 2, scale, keep_ref)


def emit(act_ref, part, z, scale, ref):
    columns = pl.ds(pl.multiple_of(part * WIDE, MAIN), WIDE)
    half = act_ref[:, columns]
    for j in range(GROUP):
        piece = half[:, j * BLK : (j + 1) * BLK]
        write(ref, jnp.bitwise_xor(z, j), pack_whole(dot(piece, piece, 0, 0) * scale, 0.0))


def statistics_plain_kernel(scale, act_ref, out_ref):
    trace = partial_trace(act_ref, scale)
    for j in range(out_ref.shape[0]):
        write(out_ref, j, pack_whole(block_statistics(act_ref, j, scale), trace))


def eliminate(tiles, count):
    lane, sub = iota((8, MAIN), 1), iota((8, MAIN), 0)

    def spread(x):
        return jnp.broadcast_to(x, (8, MAIN))

    for r in range(count // 8):
        k = 8 * r
        t = tiles[r]
        inside = (lane >= k) & (lane < k + 8)
        rows = [
            jnp.where(inside, jnp.where(lane == k + i, 1.0, 0.0), spread(t[i : i + 1, :]))
            for i in range(8)
        ]
        small = {(i, j): spread(t[i : i + 1, k + j : k + j + 1]) for i in range(8) for j in range(i, 8)}
        for a in range(8):
            pivot = 1.0 / small[a, a]
            rows[a] = rows[a] * pivot
            scaled = {b: small[a, b] * pivot for b in range(a + 1, 8)}
            for c in range(8):
                if c != a:
                    factor = small[min(a, c), max(a, c)]
                    rows[c] = rows[c] - factor * rows[a]
                    for b in range(max(a + 1, c), 8):
                        small[c, b] = small[c, b] - factor * scaled[b]
            for b in scaled:
                small[a, b] = scaled[b]
        rows = [jnp.where(inside, -x, x) for x in rows]
        for j in range(len(tiles)):
            total = None
            for i in range(8):
                if j == r:
                    column = jnp.where(sub == i, -1.0, 0.0)
                else:
                    column = spread(tiles[j][:, k + i : k + i + 1])
                total = column * rows[i] if total is None else total + column * rows[i]
            tiles[j] = -total if j == r else jnp.where(inside, 0.0, tiles[j]) - total
    return tiles


def invert(packed, level):
    b11, b21, b22 = unpack(packed)
    lane, row = iota((MAIN, MAIN), 1), iota((MAIN, MAIN), 0)
    b11 = jnp.where(lane == row, b11 + level, b11)
    tiles = [b11[8 * r : 8 * r + 8] for r in range(MAIN // 8)]
    tiles += [b21[8 * r : 8 * r + 8] for r in range(REST // 8)]
    tiles = eliminate(tiles, MAIN)
    inner = jnp.concatenate(tiles[: MAIN // 8], axis=0)
    ratio = jnp.concatenate(tiles[MAIN // 8 :], axis=0)
    lane, row = iota((REST, REST), 1), iota((REST, REST), 0)
    schur = jnp.where(lane == row, b22 + level, b22) - dot(ratio, b21, 1, 1, HIGHEST)
    schur = jnp.concatenate([schur, jnp.zeros((REST, MAIN - REST), jnp.float32)], axis=1)
    last = eliminate([schur[8 * r : 8 * r + 8] for r in range(REST // 8)], REST)
    last = -jnp.concatenate(last, axis=0)[:, :REST]
    side = dot(last, ratio, 1, 0, HIGHEST)
    return pack(dot(ratio, side, 0, 0, HIGHEST) - inner, -side, last, 0.0)


def damping(total):
    return 0.5 * total / D + 1e-06


def invert_kernel(a_ref, b_ref, c_ref, d_ref, out_ref):
    own = a_ref[0] + b_ref[0] + c_ref[0] + d_ref[0]
    trace = own[HALF + REST : HALF + REST + 1, TRACE_LANE : TRACE_LANE + 1]
    write(out_ref, 0, invert(own, damping(trace)))


def invert_plain_kernel(total_ref, in_ref, out_ref):
    write(out_ref, 0, invert(in_ref[0], damping(total_ref[0])))


def halves(packed_ref, place):
    b11, b21, b22 = unpack(packed_ref[place])
    whole = jnp.concatenate(
        [jnp.concatenate([b11, b21.T], axis=1), jnp.concatenate([b21, b22], axis=1)], axis=0
    )
    high = whole.astype(jnp.bfloat16)
    return high, (whole - high.astype(jnp.float32)).astype(jnp.bfloat16)


def build_first(packed_ref, z, top_ref, mid_ref):
    top_ref[...] = jnp.zeros_like(top_ref)
    mid_ref[...] = jnp.zeros_like(mid_ref)
    for at, part in zip((0, 384), halves(packed_ref, z)):
        top_ref[at : at + BLK, 0:BLK] = part
    for at, part in zip((0, 384), halves(packed_ref, jnp.bitwise_xor(z, 1))):
        top_ref[at + BLK : at + 2 * BLK, BLK:256] = part[:, : 256 - BLK]
    for at, part in zip((0, 512), halves(packed_ref, jnp.bitwise_xor(z, 1))):
        mid_ref[at + 32 : at + 32 + BLK, 0:64] = part[:, 96:]


def build_rest(packed_ref, z, mid_ref, end_ref):
    end_ref[...] = jnp.zeros_like(end_ref)
    for at, part in zip((0, 512), halves(packed_ref, jnp.bitwise_xor(z, 2))):
        mid_ref[at + 192 : at + 192 + BLK, 64 : 64 + BLK] = part
    for at, part in zip((0, 512), halves(packed_ref, jnp.bitwise_xor(z, 3))):
        mid_ref[at + 352 : at + 352 + BLK, 224:256] = part[:, :32]
        end_ref[96 : 96 + BLK, at // 4 : at // 4 + 128] = part[:, 32:]


def apply_kernel(first, n_groups, fetched, at_ref, *refs):
    packed = refs[:n_groups]
    if fetched:
        held = refs[n_groups : 2 * n_groups]
        out_ref, *weights, buffer, sems = refs[-9:]
        incoming = []
    else:
        out_ref, *weights, buffer, sems, room, room_sems = refs[-11:]
        held = [room.at[g] for g in range(n_groups)]
        incoming = piece_copies(at_ref, first, refs[n_groups], held, room_sems)
    z, live, start = at_ref[0], at_ref[1], at_ref[2]
    rows = held[0].shape[0]
    parts = row_parts(rows)
    keep = start + iota((rows, 1), 0) < live

    def build(g, first_part, last_part):
        top_ref, mid_ref, end_ref = weights[3 * (g % 2) : 3 * (g % 2) + 3]
        if first_part:
            build_first(packed[g], z, top_ref, mid_ref)
        if last_part:
            build_rest(packed[g], z, mid_ref, end_ref)

    def copy(g, tile):
        lo, width = 256 * tile, min(256, WIDE - 256 * tile)
        column = pl.multiple_of(at_ref[3 + first + g] * WIDE + lo, MAIN)
        return pltpu.make_async_copy(
            buffer.at[g % 2, :, lo : lo + width],
            out_ref.at[:, pl.ds(column, width)],
            sems.at[g % 2, tile],
        )

    def multiply(g):
        top_ref, mid_ref, end_ref = weights[3 * (g % 2) : 3 * (g % 2) + 3]
        if g == 0:
            build(0, True, False)
        for part in range(parts):
            here = slice(part * rows // parts, (part + 1) * rows // parts)
            left = held[g][here, 0:384]
            a = dot(jnp.concatenate([left, left], axis=1), top_ref[...], 1, 0)
            buffer[g % 2, here, 0:256] = jnp.where(keep[here], a, 0.0)
        copy(g, 0).start()
        if g == 0:
            build(0, False, True)
        if g + 1 < n_groups:
            build(g + 1, True, True)
        for part in range(parts):
            here = slice(part * rows // parts, (part + 1) * rows // parts)
            kept, right, end = keep[here], held[g][here, 128:640], held[g][here, 384:640]
            b = dot(jnp.concatenate([right, right], axis=1), mid_ref[...], 1, 0)
            buffer[g % 2, here, 256:512] = jnp.where(kept, b, 0.0)
            c = dot(end, end_ref[...], 1, 0)
            buffer[g % 2, here, 512:640] = jnp.where(kept, c[:, :128] + c[:, 128:], 0.0)
        copy(g, 1).start()
        copy(g, 2).start()

    for arrival in incoming:
        arrival.start()
    for g in range(n_groups):
        if incoming:
            incoming[g].wait()
        if g >= 2:
            for tile in range(3):
                copy(g - 2, tile).wait()
        pl.when(start >= 0)(functools.partial(multiply, g))
    for g in range(max(0, n_groups - 2), n_groups):
        for tile in range(3):
            copy(g, tile).wait()


def row_parts(rows):
    return 3 if rows % 48 == 0 else 1


def apply(groups, first, at, pieces, grad_rows, before):
    rows = grad_rows.shape[0]
    n = len(groups)
    fetched = pieces is not None
    given = pieces if fetched else [grad_rows]
    args = [*groups, *given]
    ins = [SMEM] + [VMEM] * n + ([VMEM] * n if fetched else [ANY])
    scratch = [pltpu.VMEM((k, 256), jnp.bfloat16) for k in (768, 1024, 256)] * 2
    scratch += [pltpu.VMEM((2, rows, WIDE), jnp.float32), pltpu.SemaphoreType.DMA((2, 3))]
    if not fetched:
        scratch += [pltpu.VMEM((n, rows, WIDE), grad_rows.dtype), pltpu.SemaphoreType.DMA((n,))]
    aliases = {}
    if before is not None:
        ins.append(ANY)
        args.append(before)
        aliases = {len(args): 0}
    return pl.pallas_call(
        functools.partial(apply_kernel, first, n, fetched),
        out_shape=jax.ShapeDtypeStruct((rows, D), jnp.float32),
        in_specs=ins,
        out_specs=ANY,
        scratch_shapes=scratch,
        input_output_aliases=aliases,
        compiler_params=pltpu.CompilerParams(vmem_limit_bytes=(20 if fetched else 52) << 20),
        cost_estimate=pl.CostEstimate(
            flops=4 * rows * WIDE * 256 * n, bytes_accessed=4 * rows * WIDE * n, transcendentals=0
        ),
        name="apply",
    )(at, *args)


def piece_copies(at_ref, first, grad_ref, pieces, sems):
    rows, copies = grad_ref.shape[0], []
    for g, piece in enumerate(pieces):
        column = pl.multiple_of(at_ref[3 + first + g] * WIDE, MAIN)
        source = grad_ref.at[0:rows, pl.ds(column, WIDE)]
        copies.append(pltpu.make_async_copy(source, piece, sems.at[g]))
    return copies


def fetch_kernel(at_ref, grad_ref, *refs):
    copies = piece_copies(at_ref, 0, grad_ref, refs[:-1], refs[-1])
    for copy in copies:
        copy.start()
    for copy in copies:
        copy.wait()


def swap(x, axis, mask):
    size = lax.axis_size(axis)
    return lax.ppermute(x, axis, [(i, i ^ mask) for i in range(size)])


def shards_small(activations, grad_rows, live_rows):
    scale = 1.0 / (activations.shape[0] * lax.axis_size("dp"))
    i, g = lax.axis_index("dp"), lax.axis_index("grad")
    z, y = i // 2, i % 2
    four = jax.ShapeDtypeStruct((GROUP, ROWS, MAIN), jnp.float32)
    send, trace = pl.pallas_call(
        functools.partial(send_kernel, scale),
        out_shape=(four, jax.ShapeDtypeStruct((8, MAIN), jnp.float32)),
        in_specs=[VMEM],
        out_specs=(VMEM, VMEM),
        compiler_params=SMALL,
        name="statistics_send",
    )(activations)
    received = swap(send, "dp", 1)
    keep = pl.pallas_call(
        functools.partial(keep_kernel, scale),
        out_shape=four,
        in_specs=[VMEM],
        out_specs=VMEM,
        compiler_params=SMALL,
        name="statistics_keep",
    )(activations)
    trace = trace + swap(trace, "grad", 1)
    trace = trace + swap(trace, "grad", 2)
    trace = trace + swap(trace, "dp", 1)
    half = keep + received
    half = half.at[:, HALF + REST :].add(trace[None])
    order = ((0, 0), (1, 0), (0, 1), (2, 0), (1, 1), (3, 0), (2, 1), (3, 1))
    columns = [(g ^ dg) * 2 + (y ^ dy) for dg, dy in order]
    at = jnp.stack([z, live_rows[0], i * grad_rows.shape[0], *columns]).astype(jnp.int32)
    n = 1
    pieces = pl.pallas_call(
        fetch_kernel,
        out_shape=[jax.ShapeDtypeStruct((grad_rows.shape[0], WIDE), grad_rows.dtype)] * n,
        in_specs=[SMEM, ANY],
        out_specs=[VMEM] * n,
        scratch_shapes=[pltpu.SemaphoreType.DMA((n,))],
        compiler_params=pltpu.CompilerParams(vmem_limit_bytes=50 << 20),
        cost_estimate=pl.CostEstimate(flops=0, bytes_accessed=grad_rows.size // 4, transcendentals=0),
        name="fetch",
    )(at, grad_rows)
    parts = [half[0:1], *[swap(half[e : e + 1], "dp", 2 * e) for e in range(1, 4)]]
    inverse = pl.pallas_call(
        invert_kernel,
        out_shape=jax.ShapeDtypeStruct((1, ROWS, MAIN), jnp.float32),
        in_specs=[VMEM] * 4,
        out_specs=VMEM,
        compiler_params=SMALL,
        name="invert",
    )(*parts)
    others = [swap(inverse, "dp", d) for d in (2, 4, 6)]
    others[0], pieces = lax.optimization_barrier((others[0], pieces))
    mine = jnp.concatenate([inverse, *others], axis=0)
    by_y, by_x, by_core = swap(mine, "dp", 1), swap(mine, "grad", 2), swap(mine, "grad", 1)
    out = apply([mine], 0, at, pieces, grad_rows, None)
    by_y, out = lax.optimization_barrier((by_y, out))
    by_xy = swap(by_y, "grad", 2)
    by_y_core, by_x_core = swap(by_y, "grad", 1), swap(by_x, "grad", 1)
    out = apply([by_core, by_y, by_x], 1, at, None, grad_rows, out)
    by_xy, out = lax.optimization_barrier((by_xy, out))
    by_xy_core = swap(by_xy, "grad", 1)
    return apply([by_y_core, by_x_core, by_xy, by_xy_core], 4, at, None, grad_rows, out)


def shards_any(activations, grad_rows, live_rows):
    scale = 1.0 / (activations.shape[0] * lax.axis_size("dp"))
    col_blocks = activations.shape[1] // BLK
    part = pl.pallas_call(
        functools.partial(statistics_plain_kernel, scale),
        out_shape=jax.ShapeDtypeStruct((col_blocks, ROWS, MAIN), jnp.float32),
        in_specs=[VMEM],
        out_specs=VMEM,
        name="statistics",
    )(activations)
    packed = lax.psum(part, "dp")
    total = lax.psum(packed[0, HALF + REST, TRACE_LANE].reshape(1), "grad")
    block = pl.BlockSpec((1, ROWS, MAIN), lambda b: (b, 0, 0))
    owned = pl.pallas_call(
        invert_plain_kernel,
        out_shape=jax.ShapeDtypeStruct((col_blocks, ROWS, MAIN), jnp.float32),
        grid=(col_blocks,),
        in_specs=[SMEM, block],
        out_specs=block,
        name="invert",
    )(total, packed)
    inverses = lax.all_gather(owned, "grad", axis=0, tiled=True)
    n = D // WIDE
    groups = [inverses[GROUP * j : GROUP * j + GROUP] for j in range(n)]
    start = lax.axis_index("dp") * grad_rows.shape[0]
    at = jnp.stack([jnp.int32(0), live_rows[0], start, *range(n)]).astype(jnp.int32)
    return apply(groups, 0, at, None, grad_rows, None)


def solution(mesh):
    placed = (P("dp", "grad"), P(("grad", "dp"), None), P("grad"))
    small = mesh.shape["dp"] == 8 and mesh.shape["grad"] == 4
    return jax.shard_map(
        shards_small if small else shards_any,
        mesh=mesh, in_specs=placed, out_specs=P(("grad", "dp"), None), check_vma=False,
    )
```

```python
import functools

import jax
import jax.numpy as jnp
from jax import lax
from jax.experimental import pallas as pl
from jax.experimental.pallas import tpu as pltpu
from jax.sharding import PartitionSpec as P

D = 5120
BLK = 160
MAIN = 128
REST = BLK - MAIN
HALF = 64
ROWS = 104
GROUP = 4
WIDE = GROUP * BLK
TRACE_LANE = 72
VMEM = pl.BlockSpec(memory_space=pltpu.VMEM)
ANY = pl.BlockSpec(memory_space=pl.ANY)
SMEM = pl.BlockSpec(memory_space=pltpu.SMEM)
SMALL = pltpu.CompilerParams(vmem_limit_bytes=16 << 20)
HIGHEST = lax.Precision.HIGHEST


def iota(shape, dim):
    return lax.broadcasted_iota(jnp.int32, shape, dim)


def dot(a, b, ca, cb, precision=None):
    return lax.dot_general(
        a, b, (((ca,), (cb,)), ((), ())), precision=precision, preferred_element_type=jnp.float32
    )


def pack(b11, b21, b22, trace):
    top, low = b11[:HALF], pltpu.roll(b11[HALF:], HALF, 1)
    lane, row = iota((HALF, MAIN), 1), iota((HALF, MAIN), 0)
    first = jnp.where(lane < row, low, top)
    first = jnp.where(lane < HALF, first, top)
    diagonal = jnp.sum(jnp.where(lane == row, low, 0.0), axis=1, keepdims=True)
    wide = jnp.concatenate([b22, jnp.zeros((REST, MAIN - REST), jnp.float32)], axis=1)
    lane8, row8 = iota((8, MAIN), 1), iota((8, MAIN), 0)
    corner = wide[:8]
    for m in range(1, 4):
        corner = jnp.where(lane8 // REST == m, pltpu.roll(wide[8 * m : 8 * m + 8], REST * m, 1), corner)
    for g in range(8):
        corner = jnp.where(lane8 == HALF + g, diagonal[8 * g : 8 * g + 8], corner)
    corner = jnp.where(lane8 == TRACE_LANE, jnp.where(row8 == 0, trace, 0.0), corner)
    return first, b21, corner


def unpack(packed):
    first, b21, corner = packed[:HALF], packed[HALF : HALF + REST], packed[HALF + REST :]
    turned = first.T
    lane, row = iota((HALF, HALF), 1), iota((HALF, HALF), 0)
    a, at = first[:, :HALF], turned[:HALF]
    diagonal = jnp.concatenate([corner[:, HALF + g : HALF + g + 1] for g in range(8)], axis=0)
    p = jnp.where(lane >= row, a, at)
    r = jnp.where(lane < row, a, jnp.where(lane == row, diagonal, at))
    b11 = jnp.concatenate(
        [
            jnp.concatenate([p, first[:, HALF:]], axis=1),
            jnp.concatenate([turned[HALF:], r], axis=1),
        ],
        axis=0,
    )
    b22 = jnp.concatenate([corner[:, REST * m : REST * m + REST] for m in range(4)], axis=0)
    lane, row = iota((REST, REST), 1), iota((REST, REST), 0)
    b22 = jnp.where((row >= REST // 2) & (lane < REST // 2), b22.T, b22)
    return b11, b21, b22


def block_statistics(act_ref, index, scale):
    piece = act_ref[:, index * BLK : (index + 1) * BLK]
    return dot(piece, piece, 0, 0) * scale


def partial_trace(act_ref, scale):
    x = act_ref[...].astype(jnp.float32)
    return jnp.sum(x * x) * scale


def write(ref, at, parts):
    ref[at, 0:HALF] = parts[0]
    ref[at, HALF : HALF + REST] = parts[1]
    ref[at, HALF + REST : ROWS] = parts[2]


def pack_whole(s, trace):
    return pack(s[:MAIN, :MAIN], s[MAIN:, :MAIN], s[MAIN:, MAIN:], trace)


def send_kernel(scale, act_ref, send_ref, trace_ref):
    i = lax.axis_index("dp")
    z, y = i // 2, i % 2
    emit(act_ref, 1 - y, z, scale, send_ref)
    marked = (iota((8, MAIN), 0) == 0) & (iota((8, MAIN), 1) == TRACE_LANE)
    trace_ref[...] = jnp.where(marked, partial_trace(act_ref, scale), 0.0)


def keep_kernel(scale, act_ref, keep_ref):
    i = lax.axis_index("dp")
    emit(act_ref, i % 2, i // 2, scale, keep_ref)


def emit(act_ref, part, z, scale, ref):
    columns = pl.ds(pl.multiple_of(part * WIDE, MAIN), WIDE)
    half = act_ref[:, columns]
    for j in range(GROUP):
        piece = half[:, j * BLK : (j + 1) * BLK]
        write(ref, jnp.bitwise_xor(z, j), pack_whole(dot(piece, piece, 0, 0) * scale, 0.0))


def statistics_plain_kernel(scale, act_ref, out_ref):
    trace = partial_trace(act_ref, scale)
    for j in range(out_ref.shape[0]):
        write(out_ref, j, pack_whole(block_statistics(act_ref, j, scale), trace))


def eliminate(tiles, count):
    lane, sub = iota((8, MAIN), 1), iota((8, MAIN), 0)

    def spread(x):
        return jnp.broadcast_to(x, (8, MAIN))

    for r in range(count // 8):
        k = 8 * r
        t = tiles[r]
        inside = (lane >= k) & (lane < k + 8)
        rows = [
            jnp.where(inside, jnp.where(lane == k + i, 1.0, 0.0), spread(t[i : i + 1, :]))
            for i in range(8)
        ]
        small = {(i, j): spread(t[i : i + 1, k + j : k + j + 1]) for i in range(8) for j in range(i, 8)}
        for a in range(8):
            pivot = 1.0 / small[a, a]
            rows[a] = rows[a] * pivot
            scaled = {b: small[a, b] * pivot for b in range(a + 1, 8)}
            for c in range(8):
                if c != a:
                    factor = small[min(a, c), max(a, c)]
                    rows[c] = rows[c] - factor * rows[a]
                    for b in range(max(a + 1, c), 8):
                        small[c, b] = small[c, b] - factor * scaled[b]
            for b in scaled:
                small[a, b] = scaled[b]
        rows = [jnp.where(inside, -x, x) for x in rows]
        for j in range(len(tiles)):
            total = None
            for i in range(8):
                if j == r:
                    column = jnp.where(sub == i, -1.0, 0.0)
                else:
                    column = spread(tiles[j][:, k + i : k + i + 1])
                total = column * rows[i] if total is None else total + column * rows[i]
            tiles[j] = -total if j == r else jnp.where(inside, 0.0, tiles[j]) - total
    return tiles


def invert(packed, level):
    b11, b21, b22 = unpack(packed)
    lane, row = iota((MAIN, MAIN), 1), iota((MAIN, MAIN), 0)
    b11 = jnp.where(lane == row, b11 + level, b11)
    tiles = [b11[8 * r : 8 * r + 8] for r in range(MAIN // 8)]
    tiles += [b21[8 * r : 8 * r + 8] for r in range(REST // 8)]
    tiles = eliminate(tiles, MAIN)
    inner = jnp.concatenate(tiles[: MAIN // 8], axis=0)
    ratio = jnp.concatenate(tiles[MAIN // 8 :], axis=0)
    lane, row = iota((REST, REST), 1), iota((REST, REST), 0)
    schur = jnp.where(lane == row, b22 + level, b22) - dot(ratio, b21, 1, 1, HIGHEST)
    schur = jnp.concatenate([schur, jnp.zeros((REST, MAIN - REST), jnp.float32)], axis=1)
    last = eliminate([schur[8 * r : 8 * r + 8] for r in range(REST // 8)], REST)
    last = -jnp.concatenate(last, axis=0)[:, :REST]
    side = dot(last, ratio, 1, 0, HIGHEST)
    return pack(dot(ratio, side, 0, 0, HIGHEST) - inner, -side, last, 0.0)


def damping(total):
    return 0.5 * total / D + 1e-06


def invert_kernel(a_ref, b_ref, c_ref, d_ref, out_ref):
    own = a_ref[0] + b_ref[0] + c_ref[0] + d_ref[0]
    trace = own[HALF + REST : HALF + REST + 1, TRACE_LANE : TRACE_LANE + 1]
    write(out_ref, 0, invert(own, damping(trace)))


def invert_plain_kernel(total_ref, in_ref, out_ref):
    write(out_ref, 0, invert(in_ref[0], damping(total_ref[0])))


def halves(packed_ref, place):
    b11, b21, b22 = unpack(packed_ref[place])
    whole = jnp.concatenate(
        [jnp.concatenate([b11, b21.T], axis=1), jnp.concatenate([b21, b22], axis=1)], axis=0
    )
    high = whole.astype(jnp.bfloat16)
    return high, (whole - high.astype(jnp.float32)).astype(jnp.bfloat16)


def build_first(packed_ref, z, top_ref, mid_ref):
    top_ref[...] = jnp.zeros_like(top_ref)
    mid_ref[...] = jnp.zeros_like(mid_ref)
    for at, part in zip((0, 384), halves(packed_ref, z)):
        top_ref[at : at + BLK, 0:BLK] = part
    for at, part in zip((0, 384), halves(packed_ref, jnp.bitwise_xor(z, 1))):
        top_ref[at + BLK : at + 2 * BLK, BLK:256] = part[:, : 256 - BLK]
    for at, part in zip((0, 512), halves(packed_ref, jnp.bitwise_xor(z, 1))):
        mid_ref[at + 32 : at + 32 + BLK, 0:64] = part[:, 96:]


def build_rest(packed_ref, z, mid_ref, end_ref):
    end_ref[...] = jnp.zeros_like(end_ref)
    for at, part in zip((0, 512), halves(packed_ref, jnp.bitwise_xor(z, 2))):
        mid_ref[at + 192 : at + 192 + BLK, 64 : 64 + BLK] = part
    for at, part in zip((0, 512), halves(packed_ref, jnp.bitwise_xor(z, 3))):
        mid_ref[at + 352 : at + 352 + BLK, 224:256] = part[:, :32]
        end_ref[96 : 96 + BLK, at // 4 : at // 4 + 128] = part[:, 32:]


def apply_kernel(first, n_groups, fetched, at_ref, *refs):
    packed = refs[:n_groups]
    if fetched:
        held = refs[n_groups : 2 * n_groups]
        out_ref, *weights, buffer, sems = refs[-9:]
        incoming = []
    else:
        out_ref, *weights, buffer, sems, room, room_sems = refs[-11:]
        held = [room.at[g] for g in range(n_groups)]
        incoming = piece_copies(at_ref, first, refs[n_groups], held, room_sems)
    z, live, start = at_ref[0], at_ref[1], at_ref[2]
    rows = held[0].shape[0]
    parts = row_parts(rows)
    keep = start + iota((rows, 1), 0) < live

    def build(g, first_part, last_part):
        top_ref, mid_ref, end_ref = weights[3 * (g % 2) : 3 * (g % 2) + 3]
        if first_part:
            build_first(packed[g], z, top_ref, mid_ref)
        if last_part:
            build_rest(packed[g], z, mid_ref, end_ref)

    def copy(g, tile):
        lo, width = 256 * tile, min(256, WIDE - 256 * tile)
        column = pl.multiple_of(at_ref[3 + first + g] * WIDE + lo, MAIN)
        return pltpu.make_async_copy(
            buffer.at[g % 2, :, lo : lo + width],
            out_ref.at[:, pl.ds(column, width)],
            sems.at[g % 2, tile],
        )

    def multiply(g):
        top_ref, mid_ref, end_ref = weights[3 * (g % 2) : 3 * (g % 2) + 3]

        def last_tile(kept, end, here):
            c = dot(end, end_ref[...], 1, 0)
            buffer[g % 2, here, 512:640] = jnp.where(kept, c[:, :128] + c[:, 128:], 0.0)

        if g == 0:
            build(0, True, False)
        for part in range(parts):
            here = slice(part * rows // parts, (part + 1) * rows // parts)
            left = held[g][here, 0:384]
            a = dot(jnp.concatenate([left, left], axis=1), top_ref[...], 1, 0)
            buffer[g % 2, here, 0:256] = jnp.where(keep[here], a, 0.0)
        copy(g, 0).start()
        if g == 0:
            build(0, False, True)
        if g + 1 < n_groups:
            build(g + 1, True, True)
        for part in range(parts):
            here = slice(part * rows // parts, (part + 1) * rows // parts)
            kept, right, end = keep[here], held[g][here, 128:640], held[g][here, 384:640]
            b = dot(jnp.concatenate([right, right], axis=1), mid_ref[...], 1, 0)
            buffer[g % 2, here, 256:512] = jnp.where(kept, b, 0.0)
            if g + 1 < n_groups:
                last_tile(kept, end, here)
        copy(g, 1).start()
        if g + 1 == n_groups:
            for part in range(parts):
                here = slice(part * rows // parts, (part + 1) * rows // parts)
                last_tile(keep[here], held[g][here, 384:640], here)
        copy(g, 2).start()

    for arrival in incoming:
        arrival.start()
    for g in range(n_groups):
        if incoming:
            incoming[g].wait()
        if g >= 2:
            for tile in range(3):
                copy(g - 2, tile).wait()
        pl.when(start >= 0)(functools.partial(multiply, g))
    for g in range(max(0, n_groups - 2), n_groups):
        for tile in range(3):
            copy(g, tile).wait()


def row_parts(rows):
    return 3 if rows % 48 == 0 else 1


def apply(groups, first, at, pieces, grad_rows, before):
    rows = grad_rows.shape[0]
    n = len(groups)
    fetched = pieces is not None
    given = pieces if fetched else [grad_rows]
    args = [*groups, *given]
    ins = [SMEM] + [VMEM] * n + ([VMEM] * n if fetched else [ANY])
    scratch = [pltpu.VMEM((k, 256), jnp.bfloat16) for k in (768, 1024, 256)] * 2
    scratch += [pltpu.VMEM((2, rows, WIDE), jnp.float32), pltpu.SemaphoreType.DMA((2, 3))]
    if not fetched:
        scratch += [pltpu.VMEM((n, rows, WIDE), grad_rows.dtype), pltpu.SemaphoreType.DMA((n,))]
    aliases = {}
    if before is not None:
        ins.append(ANY)
        args.append(before)
        aliases = {len(args): 0}
    return pl.pallas_call(
        functools.partial(apply_kernel, first, n, fetched),
        out_shape=jax.ShapeDtypeStruct((rows, D), jnp.float32),
        in_specs=ins,
        out_specs=ANY,
        scratch_shapes=scratch,
        input_output_aliases=aliases,
        compiler_params=pltpu.CompilerParams(vmem_limit_bytes=(20 if fetched else 52) << 20),
        cost_estimate=pl.CostEstimate(
            flops=4 * rows * WIDE * 256 * n, bytes_accessed=4 * rows * WIDE * n, transcendentals=0
        ),
        name="apply",
    )(at, *args)


def piece_copies(at_ref, first, grad_ref, pieces, sems):
    rows, copies = grad_ref.shape[0], []
    for g, piece in enumerate(pieces):
        column = pl.multiple_of(at_ref[3 + first + g] * WIDE, MAIN)
        source = grad_ref.at[0:rows, pl.ds(column, WIDE)]
        copies.append(pltpu.make_async_copy(source, piece, sems.at[g]))
    return copies


def fetch_kernel(at_ref, grad_ref, *refs):
    copies = piece_copies(at_ref, 0, grad_ref, refs[:-1], refs[-1])
    for copy in copies:
        copy.start()
    for copy in copies:
        copy.wait()


def swap(x, axis, mask):
    size = lax.axis_size(axis)
    return lax.ppermute(x, axis, [(i, i ^ mask) for i in range(size)])


def shards_small(activations, grad_rows, live_rows):
    scale = 1.0 / (activations.shape[0] * lax.axis_size("dp"))
    i, g = lax.axis_index("dp"), lax.axis_index("grad")
    z, y = i // 2, i % 2
    four = jax.ShapeDtypeStruct((GROUP, ROWS, MAIN), jnp.float32)
    send, trace = pl.pallas_call(
        functools.partial(send_kernel, scale),
        out_shape=(four, jax.ShapeDtypeStruct((8, MAIN), jnp.float32)),
        in_specs=[VMEM],
        out_specs=(VMEM, VMEM),
        compiler_params=SMALL,
        name="statistics_send",
    )(activations)
    received = swap(send, "dp", 1)
    keep = pl.pallas_call(
        functools.partial(keep_kernel, scale),
        out_shape=four,
        in_specs=[VMEM],
        out_specs=VMEM,
        compiler_params=SMALL,
        name="statistics_keep",
    )(activations)
    trace = trace + swap(trace, "grad", 1)
    trace = trace + swap(trace, "grad", 2)
    trace = trace + swap(trace, "dp", 1)
    half = keep + received
    half = half.at[:, HALF + REST :].add(trace[None])
    order = ((0, 0), (1, 0), (0, 1), (2, 0), (1, 1), (3, 0), (2, 1), (3, 1))
    columns = [(g ^ dg) * 2 + (y ^ dy) for dg, dy in order]
    at = jnp.stack([z, live_rows[0], i * grad_rows.shape[0], *columns]).astype(jnp.int32)
    n = 1
    pieces = pl.pallas_call(
        fetch_kernel,
        out_shape=[jax.ShapeDtypeStruct((grad_rows.shape[0], WIDE), grad_rows.dtype)] * n,
        in_specs=[SMEM, ANY],
        out_specs=[VMEM] * n,
        scratch_shapes=[pltpu.SemaphoreType.DMA((n,))],
        compiler_params=pltpu.CompilerParams(vmem_limit_bytes=50 << 20),
        cost_estimate=pl.CostEstimate(flops=0, bytes_accessed=grad_rows.size // 4, transcendentals=0),
        name="fetch",
    )(at, grad_rows)
    parts = [half[0:1], *[swap(half[e : e + 1], "dp", 2 * e) for e in range(1, 4)]]
    inverse = pl.pallas_call(
        invert_kernel,
        out_shape=jax.ShapeDtypeStruct((1, ROWS, MAIN), jnp.float32),
        in_specs=[VMEM] * 4,
        out_specs=VMEM,
        compiler_params=SMALL,
        name="invert",
    )(*parts)
    others = [swap(inverse, "dp", d) for d in (2, 4, 6)]
    others[0], pieces = lax.optimization_barrier((others[0], pieces))
    mine = jnp.concatenate([inverse, *others], axis=0)
    by_y, by_x, by_core = swap(mine, "dp", 1), swap(mine, "grad", 2), swap(mine, "grad", 1)
    out = apply([mine], 0, at, pieces, grad_rows, None)
    by_y, out = lax.optimization_barrier((by_y, out))
    by_xy = swap(by_y, "grad", 2)
    by_y_core, by_x_core = swap(by_y, "grad", 1), swap(by_x, "grad", 1)
    out = apply([by_core, by_y, by_x], 1, at, None, grad_rows, out)
    by_xy, out = lax.optimization_barrier((by_xy, out))
    by_xy_core = swap(by_xy, "grad", 1)
    return apply([by_y_core, by_x_core, by_xy, by_xy_core], 4, at, None, grad_rows, out)


def shards_any(activations, grad_rows, live_rows):
    scale = 1.0 / (activations.shape[0] * lax.axis_size("dp"))
    col_blocks = activations.shape[1] // BLK
    part = pl.pallas_call(
        functools.partial(statistics_plain_kernel, scale),
        out_shape=jax.ShapeDtypeStruct((col_blocks, ROWS, MAIN), jnp.float32),
        in_specs=[VMEM],
        out_specs=VMEM,
        name="statistics",
    )(activations)
    packed = lax.psum(part, "dp")
    total = lax.psum(packed[0, HALF + REST, TRACE_LANE].reshape(1), "grad")
    block = pl.BlockSpec((1, ROWS, MAIN), lambda b: (b, 0, 0))
    owned = pl.pallas_call(
        invert_plain_kernel,
        out_shape=jax.ShapeDtypeStruct((col_blocks, ROWS, MAIN), jnp.float32),
        grid=(col_blocks,),
        in_specs=[SMEM, block],
        out_specs=block,
        name="invert",
    )(total, packed)
    inverses = lax.all_gather(owned, "grad", axis=0, tiled=True)
    n = D // WIDE
    groups = [inverses[GROUP * j : GROUP * j + GROUP] for j in range(n)]
    start = lax.axis_index("dp") * grad_rows.shape[0]
    at = jnp.stack([jnp.int32(0), live_rows[0], start, *range(n)]).astype(jnp.int32)
    return apply(groups, 0, at, None, grad_rows, None)


def solution(mesh):
    placed = (P("dp", "grad"), P(("grad", "dp"), None), P("grad"))
    small = mesh.shape["dp"] == 8 and mesh.shape["grad"] == 4
    return jax.shard_map(
        shards_small if small else shards_any,
        mesh=mesh, in_specs=placed, out_specs=P(("grad", "dp"), None), check_vma=False,
    )
```
